32 devices in a mesh: ctx: 16 (over z, x, core), head: 2 (over y).
Axes of the slice: x: 2, y: 2, z: 4, core: 2. Of those that a mesh axis runs over, the one named last changes fastest.
Arguments:
- query: bfloat16 [2, 8192, 1024], P(None, 'ctx', 'head'), may hold values from -12 to 12
- key_in: bfloat16 [2, 8192, 1024], P(None, 'ctx', 'head'), may hold values from -12 to 12
- value: bfloat16 [2, 8192, 1024], P(None, 'ctx', 'head'), may hold values from -6 to 6
- rates: float32 [2, 2, 8192], P(None, 'head', 'ctx'), may hold values from 0.03 to 0.3
- w_in: bfloat16 [2, 512, 512], P('head'), may hold values from -50 to 50
- w_gate: bfloat16 [2, 512, 512], P('head'), may hold values from -50 to 50
- w_out: bfloat16 [2, 512, 512], P('head'), may hold values from -50 to 50
- norm_gain: float32 [2, 512], P('head'), may hold values from 0.1 to 1.9
- proj_weight: bfloat16 [1024, 5120], P('head'), may hold values from -0.25 to 0.25
Outputs:
- mixed: bfloat16 [2, 8192, 5120], P(None, 'ctx', 'head')
- new_in: bfloat16 [2, 512, 512], P('head')
- new_gate: bfloat16 [2, 512, 512], P('head')
- new_out: bfloat16 [2, 512, 512], P('head')
The draws below stay inside these ranges and needn't reach their ends.
All inputs are finite; a program needn't handle non-finite values.
Results may differ from the reference program's by a relative error of at most 0.015.
Values may be sent and summed in bfloat16 or wider, within the bound.
No kernel may reach another device: no remote copies, remote signals or barrier semaphores. Data moves between devices by JAX's collectives and lax.ppermute only.
A program may use at most 128 MiB of HBM per device.

```python
import math
import jax
import jax.numpy as jnp
from jax import lax

DH = 512
HID = 512
MODEL = 5120
HEADS = 2
TOKENS = 8192
GROUPS = 2
WINDOW = 1024


def paired_draw(key):
    shape_all = (GROUPS, TOKENS, HEADS * DH)
    query_part = jnp.clip(jax.random.normal(jax.random.fold_in(key, 101), shape_all, jnp.float32), -5.0, 5.0)
    key_part = jnp.clip(jax.random.normal(jax.random.fold_in(key, 102), shape_all, jnp.float32), -5.0, 5.0)
    return (query_part, key_part)


def draw_query(key, part):
    query_part, key_part = paired_draw(key)
    return query_part.astype(jnp.bfloat16)


def draw_key_in(key, part):
    query_part, key_part = paired_draw(key)
    return key_part.astype(jnp.bfloat16)


def scaled_rows(key, salt, row_count, col_count):
    normal_part = jnp.clip(jax.random.normal(jax.random.fold_in(key, salt), (HEADS, row_count, col_count), jnp.float32), -5.0, 5.0)
    position = jnp.arange(row_count, dtype=jnp.float32) / max(row_count - 1, 1)
    scales = jnp.exp(jnp.log(3.0) * position)
    return (normal_part * scales[None, :, None]).astype(jnp.bfloat16)


def draw_w_in(key, part):
    return scaled_rows(key, 201, DH, HID)


def draw_w_gate(key, part):
    return scaled_rows(key, 202, DH, HID)


def draw_w_out(key, part):
    return scaled_rows(key, 203, HID, DH)


def with_spikes(values, key, source, target, blocks, factor):
    def block_of(axis_at):
        return (jnp.arange(values.shape[axis_at]) // (values.shape[axis_at] // blocks)).reshape((-1,) + (1,) * (values.ndim - 1 - axis_at))

    near = jax.random.permutation(key, blocks)[block_of(target)]
    other_side = (block_of(target) + blocks // 2) % blocks
    return jnp.where((block_of(source) == near) | (block_of(source) == other_side), factor * values, values)


def shard_levels(own_key, dims, pieces, smallest, high):
    level = 1.0
    for dim, shards_of in pieces:
        heights = jax.random.uniform(jax.random.fold_in(jax.random.fold_in(own_key, 6), dim), (shards_of,), jnp.float32, smallest / len(pieces), high / len(pieces))
        level = level * jnp.repeat(jnp.exp(heights), dims[dim] // shards_of).reshape((-1,) + (1,) * (len(dims) - 1 - dim))
    return level


def centred(key, extent, scale, most, split=(), kind=jnp.bfloat16):
    loudness = shard_levels(key, extent, split, -0.22, 0.18) if split else 1.0
    entries = jax.random.normal(key, extent, jnp.float32) * scale * loudness
    return jnp.minimum(jnp.maximum(entries, -most), most).astype(kind)


def bell_draw_with(rng, extent, deviation, limit, split, heavy, held_as=jnp.bfloat16):
    array = deviation * jax.random.normal(rng, extent, jnp.float32)
    if split:
        array = array * shard_levels(rng, extent, split, -0.22, 0.18)
    return jnp.clip(with_spikes(array, jax.random.fold_in(rng, 3), *heavy), -limit, limit).astype(held_as)


def setup_inputs(seed: int = 0) -> dict:
    splits = jax.random.split(jax.random.key(seed), 10)
    return {
        "query": draw_query(jax.random.fold_in(splits[9], 71), 0),
        "key_in": draw_key_in(jax.random.fold_in(splits[9], 71), 0),
        "value": centred(splits[2], (GROUPS, TOKENS, HEADS * DH), 1.0, 6.0, ((1, 16), (2, 2))),
        "rates": jnp.clip(jnp.exp(math.log(0.3) - 2.3025852 * jax.random.uniform(splits[3], (GROUPS, HEADS, TOKENS), jnp.float32) ** shard_levels(splits[3], (GROUPS, HEADS, TOKENS), ((1, 2), (2, 16)), -0.2, 0.2)), 0.03, 0.3),
        "w_in": draw_w_in(jax.random.fold_in(splits[9], 71), 0),
        "w_gate": draw_w_gate(jax.random.fold_in(splits[9], 71), 0),
        "w_out": draw_w_out(jax.random.fold_in(splits[9], 71), 0),
        "norm_gain": jnp.clip(1.0 + 0.18 * jax.random.normal(splits[7], (HEADS, DH), jnp.float32), 0.1, 1.9),
        "proj_weight": bell_draw_with(splits[8], (HEADS * DH, MODEL), (HEADS * DH) ** -0.5, 0.25, ((0, 2),), (0, 1, 2, 2.0)),
    }


def silu_pair(inputs):
    sigmoid = jax.nn.sigmoid(inputs)
    return (inputs * sigmoid, sigmoid * (1.0 + inputs * (1.0 - sigmoid)))

def window_attention(query_rows, key_rows, value_rows):
    half_window = WINDOW // 2
    block = min(512, TOKENS)
    keys_pad = jnp.pad(key_rows, ((half_window, half_window), (0, 0)))
    values_pad = jnp.pad(value_rows, ((half_window, half_window), (0, 0)))
    row_ids = jnp.arange(block, dtype=jnp.int32)[:, None]
    col_ids = jnp.arange(block + WINDOW, dtype=jnp.int32)[None, :]

    def one_block(block_idx):
        offset = (block_idx * block).astype(jnp.int32)
        query_blk = lax.dynamic_slice_in_dim(query_rows, offset, block, 0)
        key_blk = lax.dynamic_slice_in_dim(keys_pad, offset, block + WINDOW, 0)
        value_blk = lax.dynamic_slice_in_dim(values_pad, offset, block + WINDOW, 0)
        scores = jnp.dot(query_blk, key_blk.T, preferred_element_type=jnp.float32) * DH ** (-0.5)
        key_glob = offset + col_ids - half_window
        valid = (col_ids - row_ids >= 0) & (col_ids - row_ids < WINDOW) & (key_glob >= 0) & (key_glob < TOKENS)
        scores = jnp.where(valid, scores, -1e+30)
        largest = lax.optimization_barrier(jnp.max(scores, axis=1, keepdims=True))
        expo = jnp.exp(scores - largest)
        probs = expo / lax.optimization_barrier(jnp.sum(expo, axis=1, keepdims=True))
        return jnp.dot(probs.astype(jnp.bfloat16), value_blk, preferred_element_type=jnp.float32)
    outputs = lax.map(one_block, jnp.arange(TOKENS // block, dtype=jnp.int32))
    return outputs.reshape(TOKENS, DH)

def head_step(inputs):
    query_rows, key_rows, value_rows, rate_row, weights_in, weights_gate, weights_out, gain_row = inputs
    scale_in = DH ** (-0.5)
    scale_out = HID ** (-0.5)
    bf_in = weights_in.astype(jnp.bfloat16)
    bf_gate = weights_gate.astype(jnp.bfloat16)
    bf_out = weights_out.astype(jnp.bfloat16)
    first_pre = jnp.dot(query_rows, bf_in, preferred_element_type=jnp.float32) * scale_in
    gate_pre = jnp.dot(query_rows, bf_gate, preferred_element_type=jnp.float32) * scale_in
    first_act, unused = silu_pair(first_pre)
    hidden_q = (first_act * gate_pre).astype(jnp.bfloat16)
    ttt_out = jnp.dot(hidden_q, bf_out, preferred_element_type=jnp.float32) * scale_out
    normed = ttt_out * lax.rsqrt(lax.optimization_barrier(jnp.mean(ttt_out * ttt_out, axis=1, keepdims=True)) + 1e-06) * gain_row[None, :]
    window = window_attention(query_rows, key_rows, value_rows)
    head_out = (normed + window).astype(jnp.bfloat16)
    key_first = jnp.dot(key_rows, bf_in, preferred_element_type=jnp.float32) * scale_in
    key_gate = jnp.dot(key_rows, bf_gate, preferred_element_type=jnp.float32) * scale_in
    key_act, key_slope = silu_pair(key_first)
    hidden_k = (key_act * key_gate).astype(jnp.bfloat16)
    scaled = (rate_row[:, None] * value_rows.astype(jnp.float32)).astype(jnp.bfloat16)
    grad_out = -scale_out * jnp.dot(hidden_k.T, scaled, preferred_element_type=jnp.float32)
    back = -scale_out * jnp.dot(scaled, bf_out.T, preferred_element_type=jnp.float32)
    delta_in = (back * key_gate * key_slope).astype(jnp.bfloat16)
    delta_gate = (back * key_act).astype(jnp.bfloat16)
    grad_in = scale_in * jnp.dot(key_rows.T, delta_in, preferred_element_type=jnp.float32)
    grad_gate = scale_in * jnp.dot(key_rows.T, delta_gate, preferred_element_type=jnp.float32)
    return (head_out, grad_in, grad_gate, grad_out)

def renormalize(updated, before):
    kept = jnp.sqrt(lax.optimization_barrier(jnp.sum(before * before, axis=-2, keepdims=True)))
    return updated * (kept / jnp.sqrt(lax.optimization_barrier(jnp.sum(updated * updated, axis=-2, keepdims=True)) + 1e-06))

def add_head(total, inputs):
    head_rows, proj_rows = inputs
    partial_value = jnp.dot(head_rows, proj_rows, preferred_element_type=jnp.float32)
    rounded = lax.optimization_barrier(partial_value.astype(jnp.bfloat16)).astype(jnp.float32)
    return (total + rounded, None)

def reference(query, key_in, value, rates, w_in, w_gate, w_out, norm_gain, proj_weight):
    state_in = w_in.astype(jnp.float32)
    state_gate = w_gate.astype(jnp.float32)
    state_out = w_out.astype(jnp.float32)
    proj_heads = proj_weight.reshape(HEADS, DH, MODEL)
    mixed_list = []
    for group_idx in range(GROUPS):
        query_heads = query[group_idx].reshape(TOKENS, HEADS, DH).transpose(1, 0, 2)
        key_heads = key_in[group_idx].reshape(TOKENS, HEADS, DH).transpose(1, 0, 2)
        value_heads = value[group_idx].reshape(TOKENS, HEADS, DH).transpose(1, 0, 2)
        head_outs, grad_in, grad_gate, grad_out = lax.map(head_step, (query_heads, key_heads, value_heads, rates[group_idx], state_in, state_gate, state_out, norm_gain))
        total, unused = lax.scan(add_head, jnp.zeros((TOKENS, MODEL), jnp.float32), (head_outs, proj_heads))
        mixed_list.append(total.astype(jnp.bfloat16))
        state_in = renormalize(state_in - grad_in, state_in)
        state_gate = renormalize(state_gate - grad_gate, state_gate)
        state_out = renormalize(state_out - grad_out, state_out)
    mixed = jnp.stack(mixed_list, axis=0)
    return (mixed, state_in.astype(jnp.bfloat16), state_gate.astype(jnp.bfloat16), state_out.astype(jnp.bfloat16))
```

```python
import functools

import jax
import jax.numpy as jnp
from jax import lax
from jax.experimental import pallas as pl
from jax.experimental.pallas import tpu as pltpu
from jax.sharding import PartitionSpec as P

GROUPS = 2
WINDOW = 1024
F32 = jnp.float32
BF16 = jnp.bfloat16
NN = (((1,), (0,)), ((), ()))
NT = (((1,), (1,)), ((), ()))
TN = (((0,), (0,)), ((), ()))


def dot(lhs, rhs, dims):
    return lax.dot_general(lhs, rhs, dims, preferred_element_type=F32)


def whole(shape):
    zeros = (0,) * len(shape)
    return pl.BlockSpec(shape, lambda i, *refs: zeros)


def of_group(group, shape):
    block = (group,) + (0,) * len(shape)
    return pl.BlockSpec((None,) + shape, lambda i, *refs: block)


ANY = pl.BlockSpec(memory_space=pl.ANY)


def key_side(core, keys, values, rate_col, weights, group, gathered):
    tokens, width = keys.shape[1:]
    hidden = width
    rows = 3 * hidden
    half = rows // 2
    step = min(256, tokens)
    scale = width ** (-0.5)
    first = NT if gathered else NN
    second = NN if gathered else NT

    def kernel(core_ref, k_ref, v_ref, rate_ref, *refs):
        if gathered:
            mine, other, send_ref, keep_ref, w_ref, hk, sc, d1, d3, grad, sems = refs
            c = core_ref[0]
            copies = (
                pltpu.make_async_copy(mine, w_ref.at[pl.ds(c * half, half)], sems.at[0]),
                pltpu.make_async_copy(other, w_ref.at[pl.ds((1 - c) * half, half)], sems.at[1]),
            )
            for copy in copies:
                copy.start()
            for copy in copies:
                copy.wait()
            w1, w3, w2 = (w_ref.at[pl.ds(n * hidden, hidden)] for n in range(3))
        else:
            w1, w3, w2, send_ref, keep_ref, hk, sc, d1, d3, grad = refs
            c = core_ref[0]

        def forward(n, carry):
            at = pl.ds(n * step, step)
            k = k_ref[at]
            f1 = dot(k, w1[...], first) * scale
            f3 = dot(k, w3[...], first) * scale
            scaled = (rate_ref[at] * v_ref[at].astype(F32)).astype(BF16)
            sc[at] = scaled
            back = dot(scaled, w2[...], second) * (-scale)
            sig = jax.nn.sigmoid(f1)
            act = f1 * sig
            slope = sig * (1.0 + f1 * (1.0 - sig))
            hk[at] = (act * f3).astype(BF16)
            d1[at] = (back * f3 * slope).astype(BF16)
            d3[at] = (back * act).astype(BF16)
            return carry

        lax.fori_loop(0, tokens // step, forward, 0)
        for n, (lhs, rhs, by) in enumerate(((d1, k_ref, scale), (d3, k_ref, scale), (sc, hk, -scale))):
            grad[pl.ds(n * hidden, hidden)] = dot(lhs[...], rhs[...], TN) * by
        send_ref[...] = grad[pl.ds(pl.multiple_of((1 - c) * half, 16), half)].astype(BF16)
        keep_ref[...] = grad[pl.ds(pl.multiple_of(c * half, 16), half)]

    act_scratch = [pltpu.VMEM((tokens, hidden), BF16) for _ in range(4)]
    scratch = act_scratch + [pltpu.VMEM((rows, width), F32)]
    if gathered:
        w_specs = [ANY, ANY]
        scratch = [pltpu.VMEM((rows, width), BF16)] + scratch + [pltpu.SemaphoreType.DMA((2,))]
    else:
        w_specs = [of_group(0, (hidden, width))] * 3
    return pl.pallas_call(
        kernel,
        grid_spec=pltpu.PrefetchScalarGridSpec(
            num_scalar_prefetch=1,
            grid=(1,),
            in_specs=[
                of_group(group, (tokens, width)),
                of_group(group, (tokens, width)),
                of_group(group, (tokens, 1)),
                *w_specs,
            ],
            out_specs=[whole((half, width)), whole((half, width))],
            scratch_shapes=scratch,
        ),
        out_shape=[
            jax.ShapeDtypeStruct((half, width), BF16),
            jax.ShapeDtypeStruct((half, width), F32),
        ],
        name="key_side",
    )(core, keys, values, rate_col, *weights)


def window_side(bounds, query, keys, values, before_k, before_v, after_k, after_v, group):
    tokens, width = query.shape[1:]
    reach = WINDOW // 2
    total = tokens + WINDOW
    step = min(256, tokens)
    span = step + WINDOW
    scale = width ** (-0.5)

    def kernel(bounds_ref, q_ref, k_ref, v_ref, bk, bv, ak, av, out_ref, k_all, v_all, sems):
        at = (pl.ds(0, reach), pl.ds(reach, tokens), pl.ds(reach + tokens, reach))
        parts = []
        for n, (source, target, place) in enumerate(
            (
                (bk.at[group], k_all, at[0]),
                (k_ref.at[group], k_all, at[1]),
                (ak.at[group], k_all, at[2]),
                (bv.at[group], v_all, at[0]),
                (v_ref.at[group], v_all, at[1]),
                (av.at[group], v_all, at[2]),
            )
        ):
            parts.append(pltpu.make_async_copy(source, target.at[place], sems.at[n]))
        for part in parts:
            part.start()
        for part in parts:
            part.wait()
        lowest, highest = bounds_ref[0], bounds_ref[1]

        def block(n, carry):
            start = n * step
            q = q_ref[pl.ds(start, step)]
            scores = dot(q, k_all[pl.ds(start, span)], NT) * scale
            row = lax.broadcasted_iota(jnp.int32, (step, span), 0)
            col = lax.broadcasted_iota(jnp.int32, (step, span), 1)
            valid = (
                (col >= row)
                & (col < row + WINDOW)
                & (col >= lowest - start)
                & (col < highest - start)
            )
            scores = jnp.where(valid, scores, -1e30)
            largest = jnp.max(scores, axis=1, keepdims=True)
            expo = jnp.exp(scores - largest)
            norm = jnp.sum(expo, axis=1, keepdims=True)
            mixed = dot(expo.astype(BF16), v_all[pl.ds(start, span)], NN)
            out_ref[pl.ds(start, step)] = mixed / norm
            return carry

        lax.fori_loop(0, tokens // step, block, 0)

    return pl.pallas_call(
        kernel,
        grid_spec=pltpu.PrefetchScalarGridSpec(
            num_scalar_prefetch=1,
            grid=(1,),
            in_specs=[of_group(group, (tokens, width))] + [ANY] * 6,
            out_specs=whole((tokens, width)),
            scratch_shapes=[
                pltpu.VMEM((total, width), BF16),
                pltpu.VMEM((total, width), BF16),
                pltpu.SemaphoreType.DMA((6,)),
            ],
        ),
        out_shape=jax.ShapeDtypeStruct((tokens, width), F32),
        name="window_side",
    )(bounds, query, keys, values, before_k, before_v, after_k, after_v)


def query_side(core, query, gain, window, weights, group, gathered):
    tokens, width = query.shape[1:]
    hidden = width
    rows = 3 * hidden
    half = rows // 2
    step = min(256, tokens)
    scale = width ** (-0.5)
    first = NT if gathered else NN

    def kernel(core_ref, q_ref, gain_ref, window_ref, *refs):
        if gathered:
            mine, other, out_ref, w_ref, sems = refs
            c = core_ref[0]
            copies = (
                pltpu.make_async_copy(mine, w_ref.at[pl.ds(c * half, half)], sems.at[0]),
                pltpu.make_async_copy(other, w_ref.at[pl.ds((1 - c) * half, half)], sems.at[1]),
            )
            for copy in copies:
                copy.start()
            for copy in copies:
                copy.wait()
            w1, w3, w2 = (w_ref.at[pl.ds(n * hidden, hidden)] for n in range(3))
        else:
            w1, w3, w2, out_ref = refs

        def block(n, carry):
            at = pl.ds(n * step, step)
            q = q_ref[at]
            g1 = dot(q, w1[...], first) * scale
            g3 = dot(q, w3[...], first) * scale
            hq = (g1 * jax.nn.sigmoid(g1) * g3).astype(BF16)
            ttt = dot(hq, w2[...], first) * scale
            mean = jnp.mean(ttt * ttt, axis=1, keepdims=True)
            normed = ttt * lax.rsqrt(mean + 1e-06) * gain_ref[...]
            out_ref[at] = (normed + window_ref[at]).astype(BF16)
            return carry

        lax.fori_loop(0, tokens // step, block, 0)

    if gathered:
        w_specs = [ANY, ANY]
        scratch = [pltpu.VMEM((rows, width), BF16), pltpu.SemaphoreType.DMA((2,))]
    else:
        w_specs = [of_group(0, (hidden, width))] * 3
        scratch = []
    return pl.pallas_call(
        kernel,
        grid_spec=pltpu.PrefetchScalarGridSpec(
            num_scalar_prefetch=1,
            grid=(1,),
            in_specs=[
                of_group(group, (tokens, width)),
                whole((1, width)),
                whole((tokens, width)),
                *w_specs,
            ],
            out_specs=whole((tokens, width)),
            scratch_shapes=scratch,
        ),
        out_shape=jax.ShapeDtypeStruct((tokens, width), BF16),
        name="query_side",
    )(core, query, gain, window, *weights)


def project(place, heads, mine, near, far, group, mixed):
    tokens, width = heads[0].shape
    count = len(heads)
    features = near[0].shape[1] if near else mine.shape[1]
    part = width // 2
    tile = 512 if features % 512 == 0 else 128

    def kernel(place_ref, *refs):
        head_refs, refs = refs[:count], refs[count:]
        mine_ref, refs = refs[0], refs[1:]
        near_refs, refs = refs[: count - 1], refs[count - 1 :]
        far_refs, refs = refs[: count - 1], refs[count - 1 :]
        out_ref = refs[-1]
        c = place_ref[0]
        total = dot(head_refs[0][...], mine_ref[...], NN)
        for head, one, two in zip(head_refs[1:], near_refs, far_refs):
            total += dot(head[:, pl.ds(pl.multiple_of(c * part, 128), part)], one[...], NN)
            total += dot(head[:, pl.ds(pl.multiple_of((1 - c) * part, 128), part)], two[...], NN)
        out_ref[...] = total.astype(BF16)

    blocks = features // tile
    operands = [*heads, mine, *near, *far]
    in_specs = [whole((tokens, width))] * count
    in_specs += [pl.BlockSpec((width, tile), lambda i, at: (0, at[1] * blocks + i))]
    in_specs += [pl.BlockSpec((part, tile), lambda i, at: (0, i))] * (2 * (count - 1))
    aliases = {}
    if mixed is not None:
        operands.append(mixed)
        in_specs.append(ANY)
        aliases = {len(operands): 0}
    return pl.pallas_call(
        kernel,
        grid_spec=pltpu.PrefetchScalarGridSpec(
            num_scalar_prefetch=1,
            grid=(blocks,),
            in_specs=in_specs,
            out_specs=pl.BlockSpec((None, tokens, tile), lambda i, at: (group, 0, i)),
        ),
        out_shape=jax.ShapeDtypeStruct((GROUPS, tokens, features), BF16),
        input_output_aliases=aliases,
        name="project",
    )(place, *operands)


def matrices(core, mine, other):
    half, width = mine.shape
    rows = 2 * half
    hidden = rows // 3

    def kernel(core_ref, mine_ref, other_ref, a, b, c, w_ref):
        core_at = core_ref[0]
        w_ref[pl.ds(pl.multiple_of(core_at * half, 16), half)] = mine_ref[...]
        w_ref[pl.ds(pl.multiple_of((1 - core_at) * half, 16), half)] = other_ref[...]
        for n, out in enumerate((a, b, c)):
            out[...] = w_ref[pl.ds(n * hidden, hidden)].T

    return pl.pallas_call(
        kernel,
        grid_spec=pltpu.PrefetchScalarGridSpec(
            num_scalar_prefetch=1,
            grid=(1,),
            in_specs=[whole((half, width))] * 2,
            out_specs=[of_group(0, (width, hidden))] * 3,
            scratch_shapes=[pltpu.VMEM((rows, width), BF16)],
        ),
        out_shape=[jax.ShapeDtypeStruct((1, width, hidden), BF16)] * 3,
        name="matrices",
    )(core, mine, other)


def orders(count):
    rest = list(range(1, count.bit_length() - 1))
    return rest, rest[1:] + rest[:1]


def exchange(value, count, step):
    even, odd = orders(count)
    pairs = [(i, i ^ (1 << (odd if i & 1 else even)[step])) for i in range(count)]
    return lax.ppermute(value, "ctx", pairs)


def own_bit(index, count, step):
    even, odd = orders(count)
    return jnp.where(index & 1, (index >> odd[step]) & 1, (index >> even[step]) & 1)


def reduce_rows(send, keep, index, count):
    swap = [(i, i ^ 1) for i in range(count)]
    got = lax.ppermute(send, "ctx", swap)
    total = keep + got.astype(F32)
    for step in range(len(orders(count)[0])):
        rows = total.shape[0] // 2
        bit = own_bit(index, count, step)
        out = lax.dynamic_slice_in_dim(total, (1 - bit) * rows, rows, 0).astype(BF16)
        got = exchange(out, count, step)
        total = lax.dynamic_slice_in_dim(total, bit * rows, rows, 0) + got.astype(F32)
    return total


def gather_rows(shard, index, count):
    for step in reversed(range(len(orders(count)[0]))):
        got = exchange(shard, count, step)
        bit = own_bit(index, count, step)
        shard = jnp.where(
            bit == 0,
            jnp.concatenate([shard, got], axis=0),
            jnp.concatenate([got, shard], axis=0),
        )
    swap = [(i, i ^ 1) for i in range(count)]
    return shard, lax.ppermute(shard, "ctx", swap)


def row_start(index, count, rows):
    rows //= 2
    start = (index & 1) * rows
    for step in range(len(orders(count)[0])):
        rows //= 2
        start += own_bit(index, count, step) * rows
    return start, rows


def renormed(before, summed):
    changed = before - summed
    kept = jnp.sqrt(jnp.sum(before * before, axis=1, keepdims=True))
    return changed * (kept / jnp.sqrt(jnp.sum(changed * changed, axis=1, keepdims=True) + 1e-06))


def local(query, key_in, value, rates, w_in, w_gate, w_out, norm_gain, proj_weight):
    count = lax.axis_size("ctx")
    heads = lax.axis_size("head")
    index = lax.axis_index("ctx")
    head = lax.axis_index("head")
    core = (index & 1).astype(jnp.int32)
    core_arg = core[None]
    tokens, width = query.shape[1:]
    reach = WINDOW // 2
    features = proj_weight.shape[1] // heads
    part = width // 2

    up = [(i, i + 1) for i in range(count - 1)]
    down = [(j, i) for i, j in up]
    before_k = lax.ppermute(key_in[:, tokens - reach :], "ctx", up)
    after_k = lax.ppermute(key_in[:, :reach], "ctx", down)
    before_v = lax.ppermute(value[:, tokens - reach :], "ctx", up)
    after_v = lax.ppermute(value[:, :reach], "ctx", down)
    bounds = jnp.stack(
        [
            jnp.where(index == 0, reach, 0),
            jnp.where(index == count - 1, reach + tokens, tokens + WINDOW),
        ]
    ).astype(jnp.int32)

    swap = [(i, i ^ 1) for i in range(count)]
    near = []
    far = []
    for shift in range(1, heads):
        target = (head + shift) % heads
        piece = lax.dynamic_slice(proj_weight, (core * part, target * features), (part, features))
        got = lax.ppermute(piece, "head", [(i, (i + shift) % heads) for i in range(heads)])
        near.append(got)
        far.append(lax.ppermute(got, "ctx", swap))
    place = jnp.stack([core, head.astype(jnp.int32)])

    natural = (w_in, w_gate, w_out)
    rate_col = rates.reshape(GROUPS, tokens, 1)
    state_rows = jnp.concatenate([w_in[0].T, w_gate[0].T, w_out[0].T], axis=0)
    start, rows = row_start(index, count, state_rows.shape[0])
    state = lax.dynamic_slice_in_dim(state_rows, start, rows, 0).astype(F32)

    weights = natural
    mixed = None
    for group in range(GROUPS):
        gathered = group > 0
        send, keep = key_side(core_arg, key_in, value, rate_col, weights, group, gathered)
        window = window_side(
            bounds, query, key_in, value, before_k, before_v, after_k, after_v, group
        )
        head_out = query_side(core_arg, query, norm_gain, window, weights, group, gathered)
        outs = [head_out]
        for shift in range(1, heads):
            outs.append(
                lax.ppermute(head_out, "head", [(i, (i + shift) % heads) for i in range(heads)])
            )
        mixed = project(place, outs, proj_weight, near, far, group, mixed)
        state = renormed(state, reduce_rows(send, keep, index, count))
        weights = gather_rows(state.astype(BF16), index, count)
    return (mixed, *matrices(core_arg, *weights))


def solution(mesh):
    return jax.shard_map(
        local,
        mesh=mesh,
        in_specs=(
            P(None, "ctx", "head"),
            P(None, "ctx", "head"),
            P(None, "ctx", "head"),
            P(None, "head", "ctx"),
            P("head", None, None),
            P("head", None, None),
            P("head", None, None),
            P("head", None),
            P("head", None),
        ),
        out_specs=(
            P(None, "ctx", "head"),
            P("head", None, None),
            P("head", None, None),
            P("head", None, None),
        ),
        check_vma=False,
    )
```

```python
import jax
import jax.numpy as jnp
from jax import lax
from jax.experimental import pallas as pl
from jax.experimental.pallas import tpu as pltpu
from jax.sharding import PartitionSpec as P


GROUPS = 2
WINDOW = 1024
F32 = jnp.float32
BF16 = jnp.bfloat16
NN = (((1,), (0,)), ((), ()))
NT = (((1,), (1,)), ((), ()))
TN = (((0,), (0,)), ((), ()))


def dot(lhs, rhs, dims):
    return lax.dot_general(lhs, rhs, dims, preferred_element_type=F32)


def whole(shape):
    zeros = (0,) * len(shape)
    return pl.BlockSpec(shape, lambda i, *refs: zeros)


HBM = pl.BlockSpec(memory_space=pltpu.HBM)
VMEM = pl.BlockSpec(memory_space=pltpu.VMEM)


def limit(mib):
    return pltpu.CompilerParams(vmem_limit_bytes=mib << 20)


def in_hbm(*arrays):
    return [pltpu.with_memory_space_constraint(array, pltpu.HBM) for array in arrays]


def fetch(pairs, sems):
    copies = [pltpu.make_async_copy(a, b, sems.at[n]) for n, (a, b) in enumerate(pairs)]
    for copy in copies:
        copy.start()
    return copies


def wait(copies):
    for copy in copies:
        copy.wait()


def weight_pairs(refs, target, hidden, gathered):
    if not gathered:
        return [(ref.at[0], target.at[pl.ds(n * hidden, hidden)]) for n, ref in enumerate(refs)]
    c = lax.axis_index("ctx") & 1
    half = target.shape[0] // 2
    return [
        (ref, target.at[pl.ds(pl.multiple_of(at * half, 16), half)])
        for ref, at in zip(refs, (c, 1 - c))
    ]


def key_side(keys, values, rates, weights, group, gathered):
    tokens, width = keys.shape[1:]
    hidden = width
    rows = 3 * hidden
    half = rows // 2
    step = min(256, tokens)
    scale = width ** (-0.5)
    first = NT if gathered else NN
    second = NN if gathered else NT
    count = len(weights)

    def kernel(k_in, v_in, rate_ref, *refs):
        w_in, refs = refs[:count], refs[count:]
        send_ref, keep_ref, *refs = refs
        stacks, refs = ([], refs) if gathered else (refs[:GROUPS], refs[GROUPS:])
        w_ref, k_all, v_all, hk, sc, d1, d3, grad, rate_col, sems, load_sems, stack_sems = refs
        loads = fetch(weight_pairs(w_in, w_ref, hidden, gathered), sems)
        wanted = [group] if gathered else list(range(GROUPS))
        wanted.sort(key=lambda g: g != group)
        fetched = fetch(
            [(a.at[g], b.at[g]) for g in wanted for a, b in ((k_in, k_all), (v_in, v_all))],
            load_sems,
        )
        w1, w3, w2 = (w_ref.at[pl.ds(n * hidden, hidden)] for n in range(3))
        k_ref, v_ref = k_all.at[group], v_all.at[group]
        rate_col[...] = jnp.broadcast_to(rate_ref[group], (8, tokens)).T
        wait(loads + fetched)
        stacking = fetch(
            [
                (source.at[g], stack.at[n])
                for g, stack in enumerate(stacks)
                for n, source in enumerate((k_all, v_all))
            ],
            stack_sems,
        )

        def forward(n, carry):
            at = pl.ds(n * step, step)
            k = k_ref[at]
            f1 = dot(k, w1[...], first) * scale
            f3 = dot(k, w3[...], first) * scale
            scaled = (rate_col[at, :1] * v_ref[at].astype(F32)).astype(BF16)
            sc[at] = scaled
            back = dot(scaled, w2[...], second) * (-scale)
            sig = jax.nn.sigmoid(f1)
            act = f1 * sig
            slope = sig * (1.0 + f1 * (1.0 - sig))
            hk[at] = (act * f3).astype(BF16)
            d1[at] = (back * f3 * slope).astype(BF16)
            d3[at] = (back * act).astype(BF16)
            return carry

        lax.fori_loop(0, tokens // step, forward, 0)
        for n, (lhs, rhs, by) in enumerate(((d1, k_ref, scale), (d3, k_ref, scale), (sc, hk, -scale))):
            grad[pl.ds(n * hidden, hidden)] = dot(lhs[...], rhs[...], TN) * by
        c = lax.axis_index("ctx") & 1
        send_ref[...] = grad[pl.ds(pl.multiple_of((1 - c) * half, 16), half)].astype(BF16)
        keep_ref[...] = grad[pl.ds(pl.multiple_of(c * half, 16), half)]
        wait(stacking)

    out_specs = [VMEM, VMEM]
    out_shape = [
        jax.ShapeDtypeStruct((half, width), BF16),
        jax.ShapeDtypeStruct((half, width), F32),
    ]
    if not gathered:
        out_specs += [HBM] * GROUPS
        out_shape += [jax.ShapeDtypeStruct((2, tokens, width), BF16)] * GROUPS
    return pl.pallas_call(
        kernel,
        in_specs=[HBM, HBM, VMEM] + [VMEM if gathered else HBM] * count,
        out_specs=out_specs,
        out_shape=out_shape,
        scratch_shapes=[
            pltpu.VMEM((rows, width), BF16),
            pltpu.VMEM((GROUPS, tokens, width), BF16),
            pltpu.VMEM((GROUPS, tokens, width), BF16),
            *[pltpu.VMEM((tokens, hidden), BF16) for _ in range(4)],
            pltpu.VMEM((rows, width), F32),
            pltpu.VMEM((tokens, 8), F32),
            pltpu.SemaphoreType.DMA((3,)),
            pltpu.SemaphoreType.DMA((2 * GROUPS,)),
            pltpu.SemaphoreType.DMA((2 * GROUPS,)),
        ],
        compiler_params=limit(28),
        name="key_side",
    )(*in_hbm(keys, values), rates, *(weights if gathered else in_hbm(*weights)))


def window_side(query, own, before, after, group):
    tokens, width = query.shape[1:]
    reach = WINDOW // 2
    total = tokens + WINDOW
    step = min(256, tokens)
    span = step + WINDOW
    scale = width ** (-0.5)

    def kernel(q_in, own_ref, before_ref, after_ref, out_ref, q_ref, k_all, v_all, sems):
        places = (pl.ds(reach, tokens), pl.ds(0, reach), pl.ds(reach + tokens, reach))
        pairs = [(q_in.at[group], q_ref)]
        for n, target in enumerate((k_all, v_all)):
            for source, place in zip((own_ref, before_ref, after_ref), places):
                pairs.append((source.at[n], target.at[place]))
        wait(fetch(pairs, sems))
        index = lax.axis_index("ctx")
        lowest = jnp.where(index == 0, reach, 0)
        highest = jnp.where(index == lax.axis_size("ctx") - 1, reach + tokens, total)

        def block(n, carry):
            start = n * step
            q = q_ref[pl.ds(start, step)]
            scores = dot(q, k_all[pl.ds(start, span)], NT) * scale
            row = lax.broadcasted_iota(jnp.int32, (step, span), 0)
            col = lax.broadcasted_iota(jnp.int32, (step, span), 1)
            valid = (
                (col >= row)
                & (col < row + WINDOW)
                & (col >= lowest - start)
                & (col < highest - start)
            )
            scores = jnp.where(valid, scores, -1e30)
            largest = jnp.max(scores, axis=1, keepdims=True)
            expo = jnp.exp(scores - largest)
            norm = jnp.sum(expo, axis=1, keepdims=True)
            mixed = dot(expo.astype(BF16), v_all[pl.ds(start, span)], NN)
            out_ref[pl.ds(start, step)] = mixed / norm
            return carry

        lax.fori_loop(0, tokens // step, block, 0)

    return pl.pallas_call(
        kernel,
        in_specs=[HBM] * 4,
        out_specs=VMEM,
        out_shape=jax.ShapeDtypeStruct((tokens, width), F32),
        scratch_shapes=[
            pltpu.VMEM((tokens, width), BF16),
            pltpu.VMEM((total, width), BF16),
            pltpu.VMEM((total, width), BF16),
            pltpu.SemaphoreType.DMA((7,)),
        ],
        compiler_params=limit(20),
        name="window_side",
    )(*in_hbm(query, own, before, after))


def query_side(query, gain, window, weights, group, gathered):
    tokens, width = query.shape[1:]
    hidden = width
    rows = 3 * hidden
    step = min(256, tokens)
    scale = width ** (-0.5)
    first = NT if gathered else NN
    count = len(weights)

    def kernel(q_in, gain_ref, window_ref, *refs):
        w_in, (out_ref, q_ref, w_ref, sems) = refs[:count], refs[count:]
        pairs = [(q_in.at[group], q_ref)]
        wait(fetch(pairs + weight_pairs(w_in, w_ref, hidden, gathered), sems))
        w1, w3, w2 = (w_ref.at[pl.ds(n * hidden, hidden)] for n in range(3))

        def block(n, carry):
            at = pl.ds(n * step, step)
            q = q_ref[at]
            g1 = dot(q, w1[...], first) * scale
            g3 = dot(q, w3[...], first) * scale
            hq = (g1 * jax.nn.sigmoid(g1) * g3).astype(BF16)
            ttt = dot(hq, w2[...], first) * scale
            mean = jnp.mean(ttt * ttt, axis=1, keepdims=True)
            normed = ttt * lax.rsqrt(mean + 1e-06) * gain_ref[...]
            out_ref[at] = (normed + window_ref[at]).astype(BF16)
            return carry

        lax.fori_loop(0, tokens // step, block, 0)

    return pl.pallas_call(
        kernel,
        in_specs=[HBM, VMEM, VMEM] + [VMEM if gathered else HBM] * count,
        out_specs=VMEM,
        out_shape=jax.ShapeDtypeStruct((tokens, width), BF16),
        scratch_shapes=[
            pltpu.VMEM((tokens, width), BF16),
            pltpu.VMEM((rows, width), BF16),
            pltpu.SemaphoreType.DMA((4,)),
        ],
        compiler_params=limit(14),
        name="query_side",
    )(*in_hbm(query), gain, window, *(weights if gathered else in_hbm(*weights)))


def project(place, heads, mine, near, far, group, mixed):
    tokens, width = heads[0].shape
    count = len(heads)
    features = near[0].shape[1] if near else mine.shape[1]
    part = width // 2
    tile = 512 if features % 512 == 0 else 128

    def kernel(place_ref, *refs):
        head_refs, refs = refs[:count], refs[count:]
        mine_ref, refs = refs[0], refs[1:]
        near_refs, refs = refs[: count - 1], refs[count - 1 :]
        far_refs, refs = refs[: count - 1], refs[count - 1 :]
        out_ref = refs[-1]
        c = place_ref[0]
        total = dot(head_refs[0][...], mine_ref[...], NN)
        for head, one, two in zip(head_refs[1:], near_refs, far_refs):
            total += dot(head[:, pl.ds(pl.multiple_of(c * part, 128), part)], one[...], NN)
            total += dot(head[:, pl.ds(pl.multiple_of((1 - c) * part, 128), part)], two[...], NN)
        out_ref[...] = total.astype(BF16)

    blocks = features // tile
    operands = [*heads, mine, *near, *far]
    in_specs = [whole((tokens, width))] * count
    in_specs += [pl.BlockSpec((width, tile), lambda i, at: (0, at[1] * blocks + i))]
    in_specs += [pl.BlockSpec((part, tile), lambda i, at: (0, i))] * (2 * (count - 1))
    aliases = {}
    if mixed is not None:
        operands.append(mixed)
        in_specs.append(HBM)
        aliases = {len(operands): 0}
    return pl.pallas_call(
        kernel,
        grid_spec=pltpu.PrefetchScalarGridSpec(
            num_scalar_prefetch=1,
            grid=(blocks,),
            in_specs=in_specs,
            out_specs=pl.BlockSpec((None, tokens, tile), lambda i, at: (group, 0, i)),
        ),
        out_shape=jax.ShapeDtypeStruct((GROUPS, tokens, features), BF16),
        input_output_aliases=aliases,
        compiler_params=limit(20),
        name="project",
    )(place, *operands)


def matrices(mine, other):
    half, width = mine.shape
    rows = 2 * half
    hidden = rows // 3

    def kernel(mine_ref, other_ref, a, b, c, w_ref, out_ref, sems, out_sems):
        wait(fetch(weight_pairs((mine_ref, other_ref), w_ref, hidden, True), sems))
        copies = []
        for n, out in enumerate((a, b, c)):
            out_ref[n] = w_ref[pl.ds(n * hidden, hidden)].T
            copies += fetch([(out_ref.at[n], out.at[0])], out_sems.at[pl.ds(n, 1)])
        wait(copies)

    return pl.pallas_call(
        kernel,
        in_specs=[VMEM] * 2,
        out_specs=[HBM] * 3,
        out_shape=[jax.ShapeDtypeStruct((1, width, hidden), BF16)] * 3,
        scratch_shapes=[
            pltpu.VMEM((rows, width), BF16),
            pltpu.VMEM((3, width, hidden), BF16),
            pltpu.SemaphoreType.DMA((2,)),
            pltpu.SemaphoreType.DMA((3,)),
        ],
        compiler_params=limit(10),
        name="matrices",
    )(mine, other)


def orders(count):
    rest = list(range(1, count.bit_length() - 1))
    return rest, rest[1:] + rest[:1]


def swap_pairs(count):
    return [(i, i ^ 1) for i in range(count)]


def exchange(value, count, step):
    even, odd = orders(count)
    pairs = [(i, i ^ (1 << (odd if i & 1 else even)[step])) for i in range(count)]
    return lax.ppermute(value, "ctx", pairs)


def own_bit(index, count, step):
    even, odd = orders(count)
    return jnp.where(index & 1, (index >> odd[step]) & 1, (index >> even[step]) & 1)


def piece_rows(refs, index, count, steps, flip):
    total = None
    for made, ref in enumerate(refs):
        start, rows = 0, ref.shape[0]
        for step in range(max(made - 1, 0), steps):
            rows //= 2
            bit = own_bit(index, count, step)
            start += (1 - bit if flip and step == steps - 1 else bit) * rows
        part = ref[...] if isinstance(start, int) else ref[pl.ds(pl.multiple_of(start, 16), rows)]
        total = part.astype(F32) if total is None else total + part.astype(F32)
    return total


def partial_sum(pieces, count, steps):
    rows, width = pieces[0].shape
    rows >>= steps

    def kernel(*refs):
        index = lax.axis_index("ctx")
        refs[-1][...] = piece_rows(refs[:-1], index, count, steps, True).astype(BF16)

    return pl.pallas_call(
        kernel,
        in_specs=[VMEM] * len(pieces),
        out_specs=VMEM,
        out_shape=jax.ShapeDtypeStruct((rows, width), BF16),
        compiler_params=limit(4),
        name="partial_sum",
    )(*pieces)


def renormed(before, pieces, count, steps):
    rows, width = before.shape

    def kernel(before_ref, *refs):
        index = lax.axis_index("ctx")
        old = before_ref[...]
        changed = old - piece_rows(refs[:-2], index, count, steps, False)
        kept = jnp.sqrt(jnp.sum(old * old, axis=1, keepdims=True))
        new = changed * (kept / jnp.sqrt(jnp.sum(changed * changed, axis=1, keepdims=True) + 1e-06))
        refs[-2][...] = new
        refs[-1][...] = new.astype(BF16)

    return pl.pallas_call(
        kernel,
        in_specs=[VMEM] * (1 + len(pieces)),
        out_specs=[VMEM] * 2,
        out_shape=[
            jax.ShapeDtypeStruct((rows, width), F32),
            jax.ShapeDtypeStruct((rows, width), BF16),
        ],
        compiler_params=limit(4),
        name="renormed",
    )(before, *pieces)


def next_state(before, send, keep, count):
    pieces = [keep, lax.ppermute(send, "ctx", swap_pairs(count))]
    steps = len(orders(count)[0])
    for step in range(steps):
        out = partial_sum(pieces, count, step + 1)
        pieces.append(exchange(out, count, step))
    return renormed(before, pieces, count, steps)


def gather_rows(shard, index, count):
    steps = len(orders(count)[0])
    for step in reversed(range(steps)):
        got = exchange(shard, count, step)
        bit = own_bit(index, count, step)
        shard = jnp.where(
            bit == 0,
            jnp.concatenate([shard, got], axis=0),
            jnp.concatenate([got, shard], axis=0),
        )
    return shard, lax.ppermute(shard, "ctx", swap_pairs(count))


def row_start(index, count, rows):
    rows //= 2
    start = (index & 1) * rows
    for step in range(len(orders(count)[0])):
        rows //= 2
        start += own_bit(index, count, step) * rows
    return start, rows


def layer(query, key_in, value, rates, w_in, w_gate, w_out, norm_gain, proj_weight):
    count = lax.axis_size("ctx")
    heads = lax.axis_size("head")
    index = lax.axis_index("ctx").astype(jnp.int32)
    head = lax.axis_index("head")
    core = (index & 1).astype(jnp.int32)
    tokens, width = query.shape[1:]
    reach = WINDOW // 2
    features = proj_weight.shape[1] // heads
    part = width // 2

    natural = (w_in, w_gate, w_out)
    send, keep, *stacks = key_side(key_in, value, rates, natural, 0, False)

    up = [(i, i + 1) for i in range(count - 1)]
    down = [(j, i) for i, j in up]
    before = []
    after = []
    for group in range(GROUPS):
        before.append(lax.ppermute(stacks[group][:, tokens - reach :], "ctx", up))
        after.append(lax.ppermute(stacks[group][:, :reach], "ctx", down))
    near = []
    far = []
    for shift in range(1, heads):
        target = (head + shift) % heads
        piece = lax.dynamic_slice(proj_weight, (core * part, target * features), (part, features))
        got = lax.ppermute(piece, "head", [(i, (i + shift) % heads) for i in range(heads)])
        near.append(got)
        far.append(lax.ppermute(got, "ctx", swap_pairs(count)))
    place = jnp.stack([core, head.astype(jnp.int32)])

    state_rows = jnp.concatenate([w_in[0].T, w_gate[0].T, w_out[0].T], axis=0)
    offset, rows = row_start(index, count, state_rows.shape[0])
    state = lax.dynamic_slice_in_dim(state_rows, offset, rows, 0).astype(F32)

    weights = natural
    mixed = None
    for group in range(GROUPS):
        gathered = group > 0
        if gathered:
            send, keep = key_side(key_in, value, rates, weights, group, True)
        window = window_side(query, stacks[group], before[group], after[group], group)
        head_out = query_side(query, norm_gain, window, weights, group, gathered)
        outs = [head_out]
        for shift in range(1, heads):
            outs.append(
                lax.ppermute(head_out, "head", [(i, (i + shift) % heads) for i in range(heads)])
            )
        mixed = project(place, outs, proj_weight, near, far, group, mixed)
        state, shard = next_state(state, send, keep, count)
        weights = gather_rows(shard, index, count)
    return (mixed, *matrices(*weights))


def solution(mesh):
    return jax.shard_map(
        layer,
        mesh=mesh,
        in_specs=(
            P(None, "ctx", "head"),
            P(None, "ctx", "head"),
            P(None, "ctx", "head"),
            P(None, "head", "ctx"),
            P("head", None, None),
            P("head", None, None),
            P("head", None, None),
            P("head", None),
            P("head", None),
        ),
        out_specs=(
            P(None, "ctx", "head"),
            P("head", None, None),
            P("head", None, None),
            P("head", None, None),
        ),
        check_vma=False,
    )
```

```python
import jax
import jax.numpy as jnp
from jax import lax
from jax.experimental import pallas as pl
from jax.experimental.pallas import tpu as pltpu
from jax.sharding import PartitionSpec as P


GROUPS = 2
WINDOW = 1024
F32 = jnp.float32
BF16 = jnp.bfloat16
NN = (((1,), (0,)), ((), ()))
NT = (((1,), (1,)), ((), ()))
TN = (((0,), (0,)), ((), ()))


def dot(lhs, rhs, dims):
    return lax.dot_general(lhs, rhs, dims, preferred_element_type=F32)


HBM = pl.BlockSpec(memory_space=pltpu.HBM)
VMEM = pl.BlockSpec(memory_space=pltpu.VMEM)


def limit(mib):
    return pltpu.CompilerParams(vmem_limit_bytes=mib << 20)


def in_hbm(*arrays):
    return [pltpu.with_memory_space_constraint(array, pltpu.HBM) for array in arrays]


def fetch(pairs, sems):
    copies = [pltpu.make_async_copy(a, b, sems.at[n]) for n, (a, b) in enumerate(pairs)]
    for copy in copies:
        copy.start()
    return copies


def wait(copies):
    for copy in copies:
        copy.wait()


def weight_pairs(refs, target, hidden, gathered):
    if not gathered:
        return [(ref.at[0], target.at[pl.ds(n * hidden, hidden)]) for n, ref in enumerate(refs)]
    c = class_of(lax.axis_index("ctx"))
    half = target.shape[0] // 2
    return [
        (ref, target.at[pl.ds(pl.multiple_of(at * half, 16), half)])
        for ref, at in zip(refs, (c, 1 - c))
    ]


def key_side(kv, rates, weights, group):
    first_group = group == 0
    tokens, width = kv.shape[1:]
    hidden = width
    rows = 3 * hidden
    half = rows // 2
    step = min(256, tokens)
    scale = width ** (-0.5)
    first = NN if first_group else NT
    second = NT if first_group else NN
    count = len(weights)

    def body(refs):
        send_ref, keep_ref, kv, w_ref, _, hk, sc, d1, d3, grad, rate_col = refs
        k_ref, v_ref = kv.at[0], kv.at[1]
        w1, w3, w2 = (w_ref.at[pl.ds(n * hidden, hidden)] for n in range(3))

        def forward(n, carry):
            at = pl.ds(n * step, step)
            k = k_ref[at]
            f1 = dot(k, w1[...], first) * scale
            f3 = dot(k, w3[...], first) * scale
            scaled = (rate_col[at, :1] * v_ref[at].astype(F32)).astype(BF16)
            sc[at] = scaled
            back = dot(scaled, w2[...], second) * (-scale)
            sig = jax.nn.sigmoid(f1)
            act = f1 * sig
            slope = sig * (1.0 + f1 * (1.0 - sig))
            hk[at] = (act * f3).astype(BF16)
            d1[at] = (back * f3 * slope).astype(BF16)
            d3[at] = (back * act).astype(BF16)
            return carry

        lax.fori_loop(0, tokens // step, forward, 0)
        for n, (lhs, rhs, by) in enumerate(((d1, k_ref, scale), (d3, k_ref, scale), (sc, hk, -scale))):
            grad[pl.ds(n * hidden, hidden)] = dot(lhs[...], rhs[...], TN) * by
        c = class_of(lax.axis_index("ctx"))
        send_ref[...] = grad[pl.ds(pl.multiple_of((1 - c) * half, 16), half)].astype(BF16)
        keep_ref[...] = grad[pl.ds(pl.multiple_of(c * half, 16), half)]

    def kernel(kv, rate_ref, *refs):
        w_in, refs = refs[:count], refs[count:]
        send_ref, keep_ref, *refs = refs
        hk, sc, d1, d3, grad, rate_col, sems, *refs = refs
        w_ref = w_in[0] if first_group else refs[0]
        rate_col[...] = jnp.broadcast_to(rate_ref[group], (8, tokens)).T
        if not first_group:
            wait(fetch(weight_pairs(w_in, w_ref, hidden, True), sems))
        body((send_ref, keep_ref, kv, w_ref, rate_ref, hk, sc, d1, d3, grad, rate_col))

    out_shape = [
        jax.ShapeDtypeStruct((half, width), BF16),
        jax.ShapeDtypeStruct((half, width), F32),
    ]
    scratch = [pltpu.VMEM((tokens, hidden), BF16) for _ in range(4)]
    scratch += [
        pltpu.VMEM((rows, width), F32),
        pltpu.VMEM((tokens, 8), F32),
        pltpu.SemaphoreType.DMA((2,)),
    ]
    operands = [kv, rates, *weights]
    in_specs = [VMEM] * len(operands)
    if not first_group:
        scratch.append(pltpu.VMEM((rows, width), BF16))
    return pl.pallas_call(
        kernel,
        in_specs=in_specs,
        out_specs=[VMEM] * len(out_shape),
        out_shape=out_shape,
        scratch_shapes=scratch,
        compiler_params=limit(12),
        name="key_side",
    )(*operands)


def side_by_side(keys, values, weights, group):
    tokens, width = keys.shape[1:]
    count = len(weights)

    def kernel(k_in, v_in, *refs):
        w_in, (kv, *w_ref, sems, w_sems) = refs[:count], refs[count:]
        loads = fetch([(k_in.at[group], kv.at[0]), (v_in.at[group], kv.at[1])], sems)
        wait(loads + (fetch(weight_pairs(w_in, w_ref[0], width, False), w_sems) if count else []))

    out_shape = [jax.ShapeDtypeStruct((2, tokens, width), BF16)]
    if count:
        out_shape.append(jax.ShapeDtypeStruct((count * width, weights[0].shape[2]), BF16))
    return pl.pallas_call(
        kernel,
        in_specs=[HBM] * (2 + count),
        out_specs=[VMEM] * len(out_shape),
        out_shape=out_shape,
        scratch_shapes=[pltpu.SemaphoreType.DMA((2,)), pltpu.SemaphoreType.DMA((3,))],
        compiler_params=limit(2),
        name="side_by_side",
    )(*in_hbm(keys, values, *weights))


def window_side(query, keys, values, chip, near, far, group):
    tokens, width = query.shape[1:]
    reach = WINDOW // 2
    total = tokens + WINDOW
    step = min(256, tokens)
    span = step + WINDOW
    scale = width ** (-0.5)

    def kernel(q_in, k_in, v_in, chip_ref, near_ref, far_ref, out_ref, q_ref, k_all, v_all, sems, far_sems):
        index = lax.axis_index("ctx")
        core = index & 1
        other = class_of(index)
        chip_at = pl.ds(pl.multiple_of((1 - core) * (reach + tokens), 128), reach)
        far_at = pl.ds(pl.multiple_of(core * (reach + tokens), 128), reach)
        pairs = [(q_in.at[group], q_ref)]
        copies = []
        for n, (own_in, target) in enumerate(((k_in, k_all), (v_in, v_all))):
            pairs.append((own_in.at[group], target.at[pl.ds(reach, tokens)]))
            pairs.append((chip_ref.at[n], target.at[chip_at]))

            @pl.when(other == 1)
            def _():
                pltpu.make_async_copy(near_ref.at[n], target.at[far_at], far_sems.at[n]).start()

            @pl.when(other == 0)
            def _():
                pltpu.make_async_copy(far_ref.at[n], target.at[far_at], far_sems.at[n]).start()

            copies.append(pltpu.make_async_copy(near_ref.at[n], target.at[far_at], far_sems.at[n]))
        wait(fetch(pairs, sems) + copies)
        lowest = jnp.where(index == 0, reach, 0)
        highest = jnp.where(index == lax.axis_size("ctx") - 1, reach + tokens, total)

        def block(n, carry):
            start = n * step
            q = q_ref[pl.ds(start, step)]
            scores = dot(q, k_all[pl.ds(start, span)], NT) * scale
            row = lax.broadcasted_iota(jnp.int32, (step, span), 0)
            col = lax.broadcasted_iota(jnp.int32, (step, span), 1)
            valid = (
                (col >= row)
                & (col < row + WINDOW)
                & (col >= lowest - start)
                & (col < highest - start)
            )
            scores = jnp.where(valid, scores, -1e30)
            largest = jnp.max(scores, axis=1, keepdims=True)
            expo = jnp.exp(scores - largest)
            norm = jnp.sum(expo, axis=1, keepdims=True)
            mixed = dot(expo.astype(BF16), v_all[pl.ds(start, span)], NN)
            out_ref[pl.ds(start, step)] = mixed / norm
            return carry

        lax.fori_loop(0, tokens // step, block, 0)

    return pl.pallas_call(
        kernel,
        in_specs=[HBM] * 6,
        out_specs=VMEM,
        out_shape=jax.ShapeDtypeStruct((tokens, width), F32),
        scratch_shapes=[
            pltpu.VMEM((tokens, width), BF16),
            pltpu.VMEM((total, width), BF16),
            pltpu.VMEM((total, width), BF16),
            pltpu.SemaphoreType.DMA((5,)),
            pltpu.SemaphoreType.DMA((2,)),
        ],
        compiler_params=limit(12),
        name="window_side",
    )(*in_hbm(query, keys, values), chip, near, far)


def query_side(query, gain, window, weights, group, gathered):
    tokens, width = query.shape[1:]
    hidden = width
    rows = 3 * hidden
    step = min(256, tokens)
    scale = width ** (-0.5)
    first = NT if gathered else NN
    count = len(weights)

    def kernel(q_in, gain_ref, window_ref, *refs):
        w_in, (out_ref, q_ref, w_ref, sems) = refs[:count], refs[count:]
        pairs = [(q_in.at[group], q_ref)]
        wait(fetch(pairs + weight_pairs(w_in, w_ref, hidden, gathered), sems))
        w1, w3, w2 = (w_ref.at[pl.ds(n * hidden, hidden)] for n in range(3))

        def block(n, carry):
            at = pl.ds(n * step, step)
            q = q_ref[at]
            g1 = dot(q, w1[...], first) * scale
            g3 = dot(q, w3[...], first) * scale
            hq = (g1 * jax.nn.sigmoid(g1) * g3).astype(BF16)
            ttt = dot(hq, w2[...], first) * scale
            mean = jnp.mean(ttt * ttt, axis=1, keepdims=True)
            normed = ttt * lax.rsqrt(mean + 1e-06) * gain_ref[...]
            out_ref[at] = (normed + window_ref[at]).astype(BF16)
            return carry

        lax.fori_loop(0, tokens // step, block, 0)

    return pl.pallas_call(
        kernel,
        in_specs=[HBM, VMEM, VMEM] + [VMEM if gathered else HBM] * count,
        out_specs=VMEM,
        out_shape=jax.ShapeDtypeStruct((tokens, width), BF16),
        scratch_shapes=[
            pltpu.VMEM((tokens, width), BF16),
            pltpu.VMEM((rows, width), BF16),
            pltpu.SemaphoreType.DMA((4,)),
        ],
        compiler_params=limit(10),
        name="query_side",
    )(*in_hbm(query), gain, window, *(weights if gathered else in_hbm(*weights)))


CALLS = 2


def tiles(features):
    tile = 512 if features % 512 == 0 else 128
    count = features // tile
    middle = (count + 1) // CALLS
    return tile, (range(middle), range(middle, count))


def project(heads, mine, near, far, group, call, mixed):
    tokens, width = heads[0].shape
    count = len(heads)
    part = width // 2
    features = mine.shape[1] // count
    tile, shares = tiles(features)
    share = shares[call]
    blocks = len(share)

    def kernel(*refs):
        head_refs, refs = refs[:count], refs[count:]
        mine_ref, refs = refs[0], refs[1:]
        near_refs, refs = refs[: count - 1], refs[count - 1 :]
        far_refs, refs = refs[: count - 1], refs[count - 1 :]
        out_ref, w_ref, done_ref, sems, out_sems = refs[-5:]
        c = lax.axis_index("ctx") & 1
        start = lax.axis_index("head") * features
        loads = fetch(
            [
                (mine_ref.at[:, pl.ds(pl.multiple_of(start + t * tile, 128), tile)], w_ref.at[n])
                for n, t in enumerate(share)
            ],
            sems,
        )
        stores = []
        for n, t in enumerate(share):
            at = pl.ds(t * tile, tile)
            total = None
            for head, one, two in zip(head_refs[1:], near_refs, far_refs):
                for source, half in ((one, c), (two, 1 - c)):
                    rows = head[:, pl.ds(pl.multiple_of(half * part, 128), part)]
                    term = dot(rows, source[:, at], NN)
                    total = term if total is None else total + term
            loads[n].wait()
            term = dot(head_refs[0][...], w_ref[n], NN)
            done_ref[n] = (term if total is None else total + term).astype(BF16)
            stores += fetch([(done_ref.at[n], out_ref.at[group, :, at])], out_sems.at[pl.ds(n, 1)])
        wait(stores)

    operands = [*heads, mine, *near, *far]
    in_specs = [VMEM] * count + [HBM] + [VMEM] * (2 * (count - 1))
    operands[count] = in_hbm(mine)[0]
    aliases = {}
    if mixed is not None:
        aliases = {len(operands): 0}
        operands.append(mixed)
        in_specs.append(HBM)
    return pl.pallas_call(
        kernel,
        in_specs=in_specs,
        out_specs=HBM,
        out_shape=jax.ShapeDtypeStruct((GROUPS, tokens, features), BF16),
        input_output_aliases=aliases,
        scratch_shapes=[
            pltpu.VMEM((blocks, width, tile), BF16),
            pltpu.VMEM((blocks, tokens, tile), BF16),
            pltpu.SemaphoreType.DMA((blocks,)),
            pltpu.SemaphoreType.DMA((blocks,)),
        ],
        compiler_params=limit(12),
        name="project",
    )(*operands)


def matrices(mine, other):
    half, width = mine.shape
    rows = 2 * half
    hidden = rows // 3

    def kernel(mine_ref, other_ref, a, b, c, w_ref, out_ref, sems, out_sems):
        wait(fetch(weight_pairs((mine_ref, other_ref), w_ref, hidden, True), sems))
        copies = []
        for n, out in enumerate((a, b, c)):
            out_ref[n] = w_ref[pl.ds(n * hidden, hidden)].T
            copies += fetch([(out_ref.at[n], out.at[0])], out_sems.at[pl.ds(n, 1)])
        wait(copies)

    return pl.pallas_call(
        kernel,
        in_specs=[VMEM] * 2,
        out_specs=[HBM] * 3,
        out_shape=[jax.ShapeDtypeStruct((1, width, hidden), BF16)] * 3,
        scratch_shapes=[
            pltpu.VMEM((rows, width), BF16),
            pltpu.VMEM((3, width, hidden), BF16),
            pltpu.SemaphoreType.DMA((2,)),
            pltpu.SemaphoreType.DMA((3,)),
        ],
        compiler_params=limit(10),
        name="matrices",
    )(mine, other)


def orders(count):
    rest = list(range(1, count.bit_length() - 1))
    return rest[1:] + rest[:1], rest


def class_of(index):
    return (index ^ (index >> 1)) & 1


def swap_pairs(count):
    return [(i, i ^ 1) for i in range(count)]


def mask(step_bit):
    return 3 if step_bit == 1 else 1 << step_bit


def exchange(value, count, step):
    ones, others = orders(count)
    pairs = [(i, i ^ mask((others if class_of(i) else ones)[step])) for i in range(count)]
    return lax.ppermute(value, "ctx", pairs)


def own_bit(index, count, step):
    ones, others = orders(count)
    return jnp.where(class_of(index) == 1, (index >> others[step]) & 1, (index >> ones[step]) & 1)


def piece_rows(refs, index, count, steps, flip):
    total = None
    for made, ref in enumerate(refs):
        start, rows = 0, ref.shape[0]
        for step in range(max(made - 1, 0), steps):
            rows //= 2
            bit = own_bit(index, count, step)
            start += (1 - bit if flip and step == steps - 1 else bit) * rows
        part = ref[...] if isinstance(start, int) else ref[pl.ds(pl.multiple_of(start, 16), rows)]
        total = part.astype(F32) if total is None else total + part.astype(F32)
    return total


def partial_sum(pieces, count, steps):
    rows, width = pieces[0].shape
    rows >>= steps

    def kernel(*refs):
        index = lax.axis_index("ctx")
        refs[-1][...] = piece_rows(refs[:-1], index, count, steps, True).astype(BF16)

    return pl.pallas_call(
        kernel,
        in_specs=[VMEM] * len(pieces),
        out_specs=VMEM,
        out_shape=jax.ShapeDtypeStruct((rows, width), BF16),
        compiler_params=limit(4),
        name="partial_sum",
    )(*pieces)


def renormed(before, pieces, count, steps):
    rows, width = before.shape

    def kernel(before_ref, *refs):
        index = lax.axis_index("ctx")
        old = before_ref[...]
        changed = old - piece_rows(refs[:-2], index, count, steps, False)
        kept = jnp.sqrt(jnp.sum(old * old, axis=1, keepdims=True))
        new = changed * (kept / jnp.sqrt(jnp.sum(changed * changed, axis=1, keepdims=True) + 1e-06))
        refs[-2][...] = new
        refs[-1][...] = new.astype(BF16)

    return pl.pallas_call(
        kernel,
        in_specs=[VMEM] * (1 + len(pieces)),
        out_specs=[VMEM] * 2,
        out_shape=[
            jax.ShapeDtypeStruct((rows, width), F32),
            jax.ShapeDtypeStruct((rows, width), BF16),
        ],
        compiler_params=limit(4),
        name="renormed",
    )(before, *pieces)


def next_state(before, send, keep, count):
    pieces = [keep, lax.ppermute(send, "ctx", swap_pairs(count))]
    steps = len(orders(count)[0])
    for step in range(steps):
        out = partial_sum(pieces, count, step + 1)
        pieces.append(exchange(out, count, step))
    return renormed(before, pieces, count, steps)


def gather_rows(shard, index, count):
    steps = len(orders(count)[0])
    for step in reversed(range(steps)):
        got = exchange(shard, count, step)
        bit = own_bit(index, count, step)
        shard = jnp.where(
            bit == 0,
            jnp.concatenate([shard, got], axis=0),
            jnp.concatenate([got, shard], axis=0),
        )
    return shard, lax.ppermute(shard, "ctx", swap_pairs(count))


def row_start(index, count, rows):
    rows //= 2
    start = class_of(index) * rows
    for step in range(len(orders(count)[0])):
        rows //= 2
        start += own_bit(index, count, step) * rows
    return start


def own_rows(weights, count):
    width, hidden = weights[0].shape[1:]
    rows = 3 * hidden

    def kernel(*refs):
        w_in, (out_ref, w_ref, turned, sems) = refs[:3], refs[3:]
        wait(fetch(weight_pairs(w_in, w_ref, width, False), sems))
        for n in range(3):
            turned[pl.ds(n * hidden, hidden)] = w_ref[pl.ds(n * width, width)].T
        start = pl.multiple_of(row_start(lax.axis_index("ctx"), count, rows), 16)
        out_ref[...] = turned[pl.ds(start, rows // count)].astype(F32)

    return pl.pallas_call(
        kernel,
        in_specs=[HBM] * 3,
        out_specs=VMEM,
        out_shape=jax.ShapeDtypeStruct((rows // count, width), F32),
        scratch_shapes=[
            pltpu.VMEM((3 * width, hidden), BF16),
            pltpu.VMEM((rows, width), BF16),
            pltpu.SemaphoreType.DMA((3,)),
        ],
        compiler_params=limit(6),
        name="own_rows",
    )(*in_hbm(*weights))


def layer(query, key_in, value, rates, w_in, w_gate, w_out, norm_gain, proj_weight):
    count = lax.axis_size("ctx")
    heads = lax.axis_size("head")
    index = lax.axis_index("ctx").astype(jnp.int32)
    head = lax.axis_index("head")
    core = (index & 1).astype(jnp.int32)
    tokens, width = query.shape[1:]
    reach = WINDOW // 2
    features = proj_weight.shape[1] // heads
    part = width // 2

    stacks = []
    for group in range(GROUPS):
        kv, *natural = side_by_side(key_in, value, () if group else (w_in, w_gate, w_out), group)
        stacks.append(kv)
        if natural:
            send, keep = key_side(kv, rates, natural, 0)

    across = [(i, i + 1 if i & 1 else i - 1) for i in range(1, count - 1)]
    near_pairs = [(i, j) for i, j in across if class_of(i)]
    far_pairs = [(i, j) for i, j in across if not class_of(i)]
    halos = []
    for own in stacks:
        to_chip = to_next = own
        if tokens > reach:
            at_end = (tokens - reach) * core
            to_next = lax.dynamic_slice_in_dim(own, at_end, reach, 1)
            to_chip = lax.dynamic_slice_in_dim(own, tokens - reach - at_end, reach, 1)
        chip = lax.ppermute(to_chip, "ctx", swap_pairs(count))
        near_halo = lax.ppermute(to_next, "ctx", near_pairs)
        far_halo = lax.ppermute(to_next, "ctx", far_pairs)
        halos.append((chip, near_halo, far_halo))

    near = []
    far = []
    for shift in range(1, heads):
        target = (head + shift) % heads
        piece = lax.dynamic_slice(proj_weight, (core * part, target * features), (part, features))
        got = lax.ppermute(piece, "head", [(i, (i + shift) % heads) for i in range(heads)])
        near.append(got)
        far.append(lax.ppermute(got, "ctx", swap_pairs(count)))

    state = own_rows((w_in, w_gate, w_out), count)

    weights = (w_in, w_gate, w_out)
    mixed = None
    for group in range(GROUPS):
        gathered = group > 0
        if gathered:
            send, keep = key_side(stacks[group], rates, weights, group)
        window = window_side(query, key_in, value, *halos[group], group)
        head_out = query_side(query, norm_gain, window, weights, group, gathered)
        outs = [head_out]
        for shift in range(1, heads):
            outs.append(
                lax.ppermute(head_out, "head", [(i, (i + shift) % heads) for i in range(heads)])
            )
        for call in range(CALLS):
            mixed = project(outs, proj_weight, near, far, group, call, mixed)
        state, shard = next_state(state, send, keep, count)
        weights = gather_rows(shard, index, count)
    return (mixed, *matrices(*weights))


def solution(mesh):
    return jax.shard_map(
        layer,
        mesh=mesh,
        in_specs=(
            P(None, "ctx", "head"),
            P(None, "ctx", "head"),
            P(None, "ctx", "head"),
            P(None, "head", "ctx"),
            P("head", None, None),
            P("head", None, None),
            P("head", None, None),
            P("head", None),
            P("head", None),
        ),
        out_specs=(
            P(None, "ctx", "head"),
            P("head", None, None),
            P("head", None, None),
            P("head", None, None),
        ),
        check_vma=False,
    )
```

```python
import jax
import jax.numpy as jnp
from jax import lax
from jax.experimental import pallas as pl
from jax.experimental.pallas import tpu as pltpu
from jax.sharding import PartitionSpec as P


GROUPS = 2
WINDOW = 1024
F32 = jnp.float32
BF16 = jnp.bfloat16
NN = (((1,), (0,)), ((), ()))
NT = (((1,), (1,)), ((), ()))
TN = (((0,), (0,)), ((), ()))


def dot(lhs, rhs, dims):
    return lax.dot_general(lhs, rhs, dims, preferred_element_type=F32)


HBM = pl.BlockSpec(memory_space=pltpu.HBM)
VMEM = pl.BlockSpec(memory_space=pltpu.VMEM)


def limit(mib):
    return pltpu.CompilerParams(vmem_limit_bytes=mib << 20)


def in_hbm(*arrays):
    return [pltpu.with_memory_space_constraint(array, pltpu.HBM) for array in arrays]


def fetch(pairs, sems):
    copies = [pltpu.make_async_copy(a, b, sems.at[n]) for n, (a, b) in enumerate(pairs)]
    for copy in copies:
        copy.start()
    return copies


def wait(copies):
    for copy in copies:
        copy.wait()


def weight_pairs(refs, target, hidden, gathered):
    if not gathered:
        return [(ref.at[0], target.at[pl.ds(n * hidden, hidden)]) for n, ref in enumerate(refs)]
    c = class_of(lax.axis_index("ctx"))
    half = target.shape[0] // 2
    return [
        (ref, target.at[pl.ds(pl.multiple_of(at * half, 16), half)])
        for ref, at in zip(refs, (c, 1 - c))
    ]


def key_side(kv, rates, weights, group):
    first_group = group == 0
    tokens, width = kv.shape[1:]
    hidden = width
    rows = 3 * hidden
    half = rows // 2
    step = min(256, tokens)
    scale = width ** (-0.5)
    first = NN if first_group else NT
    second = NT if first_group else NN
    count = len(weights)

    def body(refs):
        send_ref, keep_ref, kv, w_ref, _, hk, sc, d1, d3, grad, rate_col = refs
        k_ref, v_ref = kv.at[0], kv.at[1]
        w1, w3, w2 = (w_ref.at[pl.ds(n * hidden, hidden)] for n in range(3))

        def forward(n, carry):
            at = pl.ds(n * step, step)
            k = k_ref[at]
            f1 = dot(k, w1[...], first) * scale
            f3 = dot(k, w3[...], first) * scale
            scaled = (rate_col[at, :1] * v_ref[at].astype(F32)).astype(BF16)
            sc[at] = scaled
            back = dot(scaled, w2[...], second) * (-scale)
            sig = jax.nn.sigmoid(f1)
            act = f1 * sig
            slope = sig * (1.0 + f1 * (1.0 - sig))
            hk[at] = (act * f3).astype(BF16)
            d1[at] = (back * f3 * slope).astype(BF16)
            d3[at] = (back * act).astype(BF16)
            return carry

        lax.fori_loop(0, tokens // step, forward, 0)
        for n, (lhs, rhs, by) in enumerate(((d1, k_ref, scale), (d3, k_ref, scale), (sc, hk, -scale))):
            grad[pl.ds(n * hidden, hidden)] = dot(lhs[...], rhs[...], TN) * by
        c = class_of(lax.axis_index("ctx"))
        send_ref[...] = grad[pl.ds(pl.multiple_of((1 - c) * half, 16), half)].astype(BF16)
        keep_ref[...] = grad[pl.ds(pl.multiple_of(c * half, 16), half)]

    def kernel(kv, rate_ref, *refs):
        w_in, refs = refs[:count], refs[count:]
        send_ref, keep_ref, *refs = refs
        hk, sc, d1, d3, grad, rate_col, sems, *refs = refs
        w_ref = w_in[0] if first_group else refs[0]
        rate_col[...] = jnp.broadcast_to(rate_ref[group], (8, tokens)).T
        if not first_group:
            wait(fetch(weight_pairs(w_in, w_ref, hidden, True), sems))
        body((send_ref, keep_ref, kv, w_ref, rate_ref, hk, sc, d1, d3, grad, rate_col))

    out_shape = [
        jax.ShapeDtypeStruct((half, width), BF16),
        jax.ShapeDtypeStruct((half, width), F32),
    ]
    scratch = [pltpu.VMEM((tokens, hidden), BF16) for _ in range(4)]
    scratch += [
        pltpu.VMEM((rows, width), F32),
        pltpu.VMEM((tokens, 8), F32),
        pltpu.SemaphoreType.DMA((2,)),
    ]
    operands = [kv, rates, *weights]
    in_specs = [VMEM] * len(operands)
    if not first_group:
        scratch.append(pltpu.VMEM((rows, width), BF16))
    return pl.pallas_call(
        kernel,
        in_specs=in_specs,
        out_specs=[VMEM] * len(out_shape),
        out_shape=out_shape,
        scratch_shapes=scratch,
        compiler_params=limit(12),
        name="key_side",
    )(*operands)


def side_by_side(keys, values, weights, group, singles):
    tokens, width = keys.shape[1:]
    count = len(weights)
    sources = [(0, group), (1, group), *singles]

    def kernel(*refs):
        kv_in, w_in, refs = refs[:2], refs[2 : 2 + count], refs[2 + count :]
        kv, targets, (*w_ref, sems, w_sems) = refs[0], refs[1 : 1 + len(singles)], refs[1 + len(singles) :]
        targets = (kv.at[0], kv.at[1], *targets)
        loads = fetch([(kv_in[n].at[g], to) for (n, g), to in zip(sources, targets)], sems)
        wait(loads + (fetch(weight_pairs(w_in, w_ref[0], width, False), w_sems) if count else []))

    out_shape = [jax.ShapeDtypeStruct((2, tokens, width), BF16)]
    out_shape += [jax.ShapeDtypeStruct((tokens, width), BF16)] * len(singles)
    if count:
        out_shape.append(jax.ShapeDtypeStruct((count * width, weights[0].shape[2]), BF16))
    return pl.pallas_call(
        kernel,
        in_specs=[HBM] * (2 + count),
        out_specs=[VMEM] * len(out_shape),
        out_shape=out_shape,
        scratch_shapes=[pltpu.SemaphoreType.DMA((len(sources),)), pltpu.SemaphoreType.DMA((3,))],
        compiler_params=limit(2),
        name="side_by_side",
    )(*in_hbm(keys, values, *weights))


def window_side(query, keys, values, chip, near, far, group):
    tokens, width = query.shape[1:]
    reach = WINDOW // 2
    total = tokens + WINDOW
    step = min(256, tokens)
    span = step + WINDOW
    scale = width ** (-0.5)

    def kernel(q_in, k_in, v_in, chip_ref, near_ref, *refs):
        far_refs, (out_ref, q_ref, k_all, v_all, sems, far_sems) = refs[:-6], refs[-6:]
        far_parts = far_refs if len(far_refs) == 2 else (far_refs[0].at[0], far_refs[0].at[1])
        index = lax.axis_index("ctx")
        core = index & 1
        other = class_of(index)
        chip_at = pl.ds(pl.multiple_of((1 - core) * (reach + tokens), 128), reach)
        far_at = pl.ds(pl.multiple_of(core * (reach + tokens), 128), reach)
        pairs = [(q_in.at[group], q_ref)]
        copies = []
        for n, (own_in, target) in enumerate(((k_in, k_all), (v_in, v_all))):
            pairs.append((own_in.at[group], target.at[pl.ds(reach, tokens)]))
            pairs.append((chip_ref.at[n], target.at[chip_at]))

            @pl.when(other == 1)
            def _():
                pltpu.make_async_copy(near_ref.at[n], target.at[far_at], far_sems.at[n]).start()

            @pl.when(other == 0)
            def _():
                pltpu.make_async_copy(far_parts[n], target.at[far_at], far_sems.at[n]).start()

            copies.append(pltpu.make_async_copy(near_ref.at[n], target.at[far_at], far_sems.at[n]))
        wait(fetch(pairs, sems) + copies)
        lowest = jnp.where(index == 0, reach, 0)
        highest = jnp.where(index == lax.axis_size("ctx") - 1, reach + tokens, total)

        def block(n, carry):
            start = n * step
            q = q_ref[pl.ds(start, step)]
            scores = dot(q, k_all[pl.ds(start, span)], NT) * scale
            row = lax.broadcasted_iota(jnp.int32, (step, span), 0)
            col = lax.broadcasted_iota(jnp.int32, (step, span), 1)
            valid = (
                (col >= row)
                & (col < row + WINDOW)
                & (col >= lowest - start)
                & (col < highest - start)
            )
            scores = jnp.where(valid, scores, -1e30)
            largest = jnp.max(scores, axis=1, keepdims=True)
            expo = jnp.exp(scores - largest)
            norm = jnp.sum(expo, axis=1, keepdims=True)
            mixed = dot(expo.astype(BF16), v_all[pl.ds(start, span)], NN)
            out_ref[pl.ds(start, step)] = mixed / norm
            return carry

        lax.fori_loop(0, tokens // step, block, 0)

    return pl.pallas_call(
        kernel,
        in_specs=[HBM] * (5 + len(far)),
        out_specs=VMEM,
        out_shape=jax.ShapeDtypeStruct((tokens, width), F32),
        scratch_shapes=[
            pltpu.VMEM((tokens, width), BF16),
            pltpu.VMEM((total, width), BF16),
            pltpu.VMEM((total, width), BF16),
            pltpu.SemaphoreType.DMA((5,)),
            pltpu.SemaphoreType.DMA((2,)),
        ],
        compiler_params=limit(12),
        name="window_side",
    )(*in_hbm(query, keys, values), chip, near, *far)


def query_side(query, gain, window, weights, group, gathered):
    tokens, width = query.shape[1:]
    hidden = width
    rows = 3 * hidden
    step = min(256, tokens)
    scale = width ** (-0.5)
    first = NT if gathered else NN
    count = len(weights)

    def kernel(q_in, gain_ref, window_ref, *refs):
        w_in, (out_ref, q_ref, w_ref, sems) = refs[:count], refs[count:]
        pairs = [(q_in.at[group], q_ref)]
        wait(fetch(pairs + weight_pairs(w_in, w_ref, hidden, gathered), sems))
        w1, w3, w2 = (w_ref.at[pl.ds(n * hidden, hidden)] for n in range(3))

        def block(n, carry):
            at = pl.ds(n * step, step)
            q = q_ref[at]
            g1 = dot(q, w1[...], first) * scale
            g3 = dot(q, w3[...], first) * scale
            hq = (g1 * jax.nn.sigmoid(g1) * g3).astype(BF16)
            ttt = dot(hq, w2[...], first) * scale
            mean = jnp.mean(ttt * ttt, axis=1, keepdims=True)
            normed = ttt * lax.rsqrt(mean + 1e-06) * gain_ref[...]
            out_ref[at] = (normed + window_ref[at]).astype(BF16)
            return carry

        lax.fori_loop(0, tokens // step, block, 0)

    return pl.pallas_call(
        kernel,
        in_specs=[HBM, VMEM, VMEM] + [VMEM if gathered else HBM] * count,
        out_specs=VMEM,
        out_shape=jax.ShapeDtypeStruct((tokens, width), BF16),
        scratch_shapes=[
            pltpu.VMEM((tokens, width), BF16),
            pltpu.VMEM((rows, width), BF16),
            pltpu.SemaphoreType.DMA((4,)),
        ],
        compiler_params=limit(10),
        name="query_side",
    )(*in_hbm(query), gain, window, *(weights if gathered else in_hbm(*weights)))


CALLS = 2


def tiles(features):
    tile = 512 if features % 512 == 0 else 128
    count = features // tile
    middle = (count + 1) // CALLS
    return tile, (range(middle), range(middle, count))


def project(heads, mine, near, far, group, call, mixed):
    tokens, width = heads[0].shape
    count = len(heads)
    part = width // 2
    features = mine.shape[1] // count
    tile, shares = tiles(features)
    share = shares[call]
    blocks = len(share)

    def kernel(*refs):
        head_refs, refs = refs[:count], refs[count:]
        mine_ref, refs = refs[0], refs[1:]
        near_refs, refs = refs[: count - 1], refs[count - 1 :]
        far_refs, refs = refs[: count - 1], refs[count - 1 :]
        out_ref, w_ref, done_ref, sems, out_sems = refs[-5:]
        c = lax.axis_index("ctx") & 1
        start = lax.axis_index("head") * features
        loads = fetch(
            [
                (mine_ref.at[:, pl.ds(pl.multiple_of(start + t * tile, 128), tile)], w_ref.at[n])
                for n, t in enumerate(share)
            ],
            sems,
        )
        stores = []
        for n, t in enumerate(share):
            at = pl.ds(t * tile, tile)
            total = None
            for head, one, two in zip(head_refs[1:], near_refs, far_refs):
                for source, half in ((one, c), (two, 1 - c)):
                    rows = head[:, pl.ds(pl.multiple_of(half * part, 128), part)]
                    term = dot(rows, source[:, at], NN)
                    total = term if total is None else total + term
            loads[n].wait()
            term = dot(head_refs[0][...], w_ref[n], NN)
            done_ref[n] = (term if total is None else total + term).astype(BF16)
            stores += fetch([(done_ref.at[n], out_ref.at[group, :, at])], out_sems.at[pl.ds(n, 1)])
        wait(stores)

    operands = [*heads, mine, *near, *far]
    in_specs = [VMEM] * count + [HBM] + [VMEM] * (2 * (count - 1))
    operands[count] = in_hbm(mine)[0]
    aliases = {}
    if mixed is not None:
        aliases = {len(operands): 0}
        operands.append(mixed)
        in_specs.append(HBM)
    return pl.pallas_call(
        kernel,
        in_specs=in_specs,
        out_specs=HBM,
        out_shape=jax.ShapeDtypeStruct((GROUPS, tokens, features), BF16),
        input_output_aliases=aliases,
        scratch_shapes=[
            pltpu.VMEM((blocks, width, tile), BF16),
            pltpu.VMEM((blocks, tokens, tile), BF16),
            pltpu.SemaphoreType.DMA((blocks,)),
            pltpu.SemaphoreType.DMA((blocks,)),
        ],
        compiler_params=limit(12),
        name="project",
    )(*operands)


def piece_for(weights, shift, heads):
    width, features = weights.shape
    part = width // 2
    features //= heads

    def kernel(in_ref, out_ref, sem):
        c = lax.axis_index("ctx") & 1
        target = (lax.axis_index("head") + shift) % heads
        rows = pl.ds(pl.multiple_of(c * part, 16), part)
        columns = pl.ds(pl.multiple_of(target * features, 128), features)
        wait(fetch([(in_ref.at[rows, columns], out_ref)], sem))

    return pl.pallas_call(
        kernel,
        in_specs=[HBM],
        out_specs=VMEM,
        out_shape=jax.ShapeDtypeStruct((part, features), weights.dtype),
        scratch_shapes=[pltpu.SemaphoreType.DMA((1,))],
        compiler_params=limit(2),
        name="piece_for",
    )(*in_hbm(weights))


def matrices(mine, other):
    half, width = mine.shape
    rows = 2 * half
    hidden = rows // 3

    def kernel(mine_ref, other_ref, a, b, c, w_ref, out_ref, sems, out_sems):
        wait(fetch(weight_pairs((mine_ref, other_ref), w_ref, hidden, True), sems))
        copies = []
        for n, out in enumerate((a, b, c)):
            out_ref[n] = w_ref[pl.ds(n * hidden, hidden)].T
            copies += fetch([(out_ref.at[n], out.at[0])], out_sems.at[pl.ds(n, 1)])
        wait(copies)

    return pl.pallas_call(
        kernel,
        in_specs=[VMEM] * 2,
        out_specs=[HBM] * 3,
        out_shape=[jax.ShapeDtypeStruct((1, width, hidden), BF16)] * 3,
        scratch_shapes=[
            pltpu.VMEM((rows, width), BF16),
            pltpu.VMEM((3, width, hidden), BF16),
            pltpu.SemaphoreType.DMA((2,)),
            pltpu.SemaphoreType.DMA((3,)),
        ],
        compiler_params=limit(10),
        name="matrices",
    )(mine, other)


def orders(count):
    rest = list(range(1, count.bit_length() - 1))
    return rest[1:] + rest[:1], rest


def class_of(index):
    return (index ^ (index >> 1)) & 1


def swap_pairs(count):
    return [(i, i ^ 1) for i in range(count)]


def mask(step_bit):
    return 3 if step_bit == 1 else 1 << step_bit


def exchange(value, count, step):
    ones, others = orders(count)
    pairs = [(i, i ^ mask((others if class_of(i) else ones)[step])) for i in range(count)]
    return lax.ppermute(value, "ctx", pairs)


def own_bit(index, count, step):
    ones, others = orders(count)
    return jnp.where(class_of(index) == 1, (index >> others[step]) & 1, (index >> ones[step]) & 1)


def piece_rows(refs, index, count, steps, flip):
    total = None
    for made, ref in enumerate(refs):
        start, rows = 0, ref.shape[0]
        for step in range(max(made - 1, 0), steps):
            rows //= 2
            bit = own_bit(index, count, step)
            start += (1 - bit if flip and step == steps - 1 else bit) * rows
        part = ref[...] if isinstance(start, int) else ref[pl.ds(pl.multiple_of(start, 16), rows)]
        total = part.astype(F32) if total is None else total + part.astype(F32)
    return total


def partial_sum(pieces, count, steps):
    rows, width = pieces[0].shape
    rows >>= steps

    def kernel(*refs):
        index = lax.axis_index("ctx")
        refs[-1][...] = piece_rows(refs[:-1], index, count, steps, True).astype(BF16)

    return pl.pallas_call(
        kernel,
        in_specs=[VMEM] * len(pieces),
        out_specs=VMEM,
        out_shape=jax.ShapeDtypeStruct((rows, width), BF16),
        compiler_params=limit(4),
        name="partial_sum",
    )(*pieces)


def renormed(before, pieces, count, steps):
    rows, width = before.shape

    def kernel(before_ref, *refs):
        index = lax.axis_index("ctx")
        old = before_ref[...]
        changed = old - piece_rows(refs[:-2], index, count, steps, False)
        kept = jnp.sqrt(jnp.sum(old * old, axis=1, keepdims=True))
        new = changed * (kept / jnp.sqrt(jnp.sum(changed * changed, axis=1, keepdims=True) + 1e-06))
        refs[-2][...] = new
        refs[-1][...] = new.astype(BF16)

    return pl.pallas_call(
        kernel,
        in_specs=[VMEM] * (1 + len(pieces)),
        out_specs=[VMEM] * 2,
        out_shape=[
            jax.ShapeDtypeStruct((rows, width), F32),
            jax.ShapeDtypeStruct((rows, width), BF16),
        ],
        compiler_params=limit(4),
        name="renormed",
    )(before, *pieces)


def next_state(before, send, keep, count):
    pieces = [keep, lax.ppermute(send, "ctx", swap_pairs(count))]
    steps = len(orders(count)[0])
    for step in range(steps):
        out = partial_sum(pieces, count, step + 1)
        pieces.append(exchange(out, count, step))
    return renormed(before, pieces, count, steps)


def joined(shard, got, count, step):
    rows, width = shard.shape

    def kernel(shard_ref, got_ref, out_ref):
        bit = own_bit(lax.axis_index("ctx"), count, step)
        out_ref[pl.ds(pl.multiple_of(bit * rows, 16), rows)] = shard_ref[...]
        out_ref[pl.ds(pl.multiple_of((1 - bit) * rows, 16), rows)] = got_ref[...]

    return pl.pallas_call(
        kernel,
        in_specs=[VMEM] * 2,
        out_specs=VMEM,
        out_shape=jax.ShapeDtypeStruct((2 * rows, width), shard.dtype),
        compiler_params=limit(4),
        name="joined",
    )(shard, got)


def gather_rows(shard, count):
    steps = len(orders(count)[0])
    for step in reversed(range(steps)):
        got = exchange(shard, count, step)
        shard = joined(shard, got, count, step)
    return shard, lax.ppermute(shard, "ctx", swap_pairs(count))


def row_start(index, count, rows):
    rows //= 2
    start = class_of(index) * rows
    for step in range(len(orders(count)[0])):
        rows //= 2
        start += own_bit(index, count, step) * rows
    return start


def own_rows(weights, count):
    width, hidden = weights[0].shape[1:]
    rows = 3 * hidden

    def kernel(*refs):
        w_in, (out_ref, w_ref, turned, sems) = refs[:3], refs[3:]
        wait(fetch(weight_pairs(w_in, w_ref, width, False), sems))
        for n in range(3):
            turned[pl.ds(n * hidden, hidden)] = w_ref[pl.ds(n * width, width)].T
        start = pl.multiple_of(row_start(lax.axis_index("ctx"), count, rows), 16)
        out_ref[...] = turned[pl.ds(start, rows // count)].astype(F32)

    return pl.pallas_call(
        kernel,
        in_specs=[HBM] * 3,
        out_specs=VMEM,
        out_shape=jax.ShapeDtypeStruct((rows // count, width), F32),
        scratch_shapes=[
            pltpu.VMEM((3 * width, hidden), BF16),
            pltpu.VMEM((rows, width), BF16),
            pltpu.SemaphoreType.DMA((3,)),
        ],
        compiler_params=limit(6),
        name="own_rows",
    )(*in_hbm(*weights))


def layer(query, key_in, value, rates, w_in, w_gate, w_out, norm_gain, proj_weight):
    count = lax.axis_size("ctx")
    heads = lax.axis_size("head")
    index = lax.axis_index("ctx").astype(jnp.int32)
    core = (index & 1).astype(jnp.int32)
    tokens, _ = query.shape[1:]
    reach = WINDOW // 2

    kv, keys_only, natural = side_by_side(key_in, value, (w_in, w_gate, w_out), 0, [(0, 0)])
    send, keep = key_side(kv, rates, [natural], 0)
    later, values_only = side_by_side(key_in, value, (), 1, [(1, 0)])

    across = [(i, i + 1 if i & 1 else i - 1) for i in range(1, count - 1)]
    near_pairs = [(i, j) for i, j in across if class_of(i)]
    far_pairs = [(i, j) for i, j in across if not class_of(i)]

    def edge(rows, at_end):
        axis = rows.ndim - 2
        if tokens == reach:
            return rows
        return lax.dynamic_slice_in_dim(rows, (tokens - reach) * at_end, reach, axis)

    halos = []
    for own, alone in ((kv, (keys_only, values_only)), (later, (later,))):
        chip = lax.ppermute(edge(own, 1 - core), "ctx", swap_pairs(count))
        near_halo = lax.ppermute(edge(own, core), "ctx", near_pairs)
        far_halo = []
        for rows in alone:
            far_halo.append(lax.ppermute(edge(rows, core), "ctx", far_pairs))
        halos.append((chip, near_halo, far_halo))

    near = []
    far = []
    for shift in range(1, heads):
        piece = piece_for(proj_weight, shift, heads)
        got = lax.ppermute(piece, "head", [(i, (i + shift) % heads) for i in range(heads)])
        near.append(got)
        far.append(lax.ppermute(got, "ctx", swap_pairs(count)))

    state = own_rows((w_in, w_gate, w_out), count)

    weights = (w_in, w_gate, w_out)
    mixed = None
    for group in range(GROUPS):
        gathered = group > 0
        if gathered:
            send, keep = key_side(later, rates, weights, group)
        window = window_side(query, key_in, value, *halos[group], group)
        head_out = query_side(query, norm_gain, window, weights, group, gathered)
        outs = [head_out]
        for shift in range(1, heads):
            outs.append(
                lax.ppermute(head_out, "head", [(i, (i + shift) % heads) for i in range(heads)])
            )
        for call in range(CALLS):
            mixed = project(outs, proj_weight, near, far, group, call, mixed)
        state, shard = next_state(state, send, keep, count)
        weights = gather_rows(shard, count)
    return (mixed, *matrices(*weights))


def solution(mesh):
    return jax.shard_map(
        layer,
        mesh=mesh,
        in_specs=(
            P(None, "ctx", "head"),
            P(None, "ctx", "head"),
            P(None, "ctx", "head"),
            P(None, "head", "ctx"),
            P("head", None, None),
            P("head", None, None),
            P("head", None, None),
            P("head", None),
            P("head", None),
        ),
        out_specs=(
            P(None, "ctx", "head"),
            P("head", None, None),
            P("head", None, None),
            P("head", None, None),
        ),
        check_vma=False,
    )
```

```python
import jax
import jax.numpy as jnp
from jax import lax
from jax.experimental import pallas as pl
from jax.experimental.pallas import tpu as pltpu
from jax.sharding import PartitionSpec as P


GROUPS = 2
WINDOW = 1024
F32 = jnp.float32
BF16 = jnp.bfloat16
NN = (((1,), (0,)), ((), ()))
NT = (((1,), (1,)), ((), ()))
TN = (((0,), (0,)), ((), ()))


def dot(lhs, rhs, dims):
    return lax.dot_general(lhs, rhs, dims, preferred_element_type=F32)


HBM = pl.BlockSpec(memory_space=pltpu.HBM)
VMEM = pl.BlockSpec(memory_space=pltpu.VMEM)


def limit(mib):
    return pltpu.CompilerParams(vmem_limit_bytes=mib << 20)


def in_hbm(*arrays):
    return [pltpu.with_memory_space_constraint(array, pltpu.HBM) for array in arrays]


def fetch(pairs, sems):
    copies = [pltpu.make_async_copy(a, b, sems.at[n]) for n, (a, b) in enumerate(pairs)]
    for copy in copies:
        copy.start()
    return copies


def wait(copies):
    for copy in copies:
        copy.wait()


def weight_pairs(refs, target, hidden, gathered):
    if not gathered:
        return [(ref.at[0], target.at[pl.ds(n * hidden, hidden)]) for n, ref in enumerate(refs)]
    c = class_of(lax.axis_index("ctx"))
    half = target.shape[0] // 2
    return [
        (ref, target.at[pl.ds(pl.multiple_of(at * half, 16), half)])
        for ref, at in zip(refs, (c, 1 - c))
    ]


def key_side(kv, rates, weights, group):
    first_group = group == 0
    tokens, width = kv.shape[1:]
    hidden = width
    rows = 3 * hidden
    half = rows // 2
    step = min(512, tokens)
    scale = width ** (-0.5)
    first = NN if first_group else NT
    second = NT if first_group else NN
    count = len(weights)

    def body(refs):
        send_ref, keep_ref, kv, w_ref, _, hk, sc, d1, d3, grad, rate_col = refs
        k_ref, v_ref = kv.at[0], kv.at[1]
        w1, w3, w2 = (w_ref.at[pl.ds(n * hidden, hidden)] for n in range(3))

        def forward(n, carry):
            at = pl.ds(n * step, step)
            k = k_ref[at]
            f1 = dot(k, w1[...], first) * scale
            f3 = dot(k, w3[...], first) * scale
            scaled = (rate_col[at, :1] * v_ref[at].astype(F32)).astype(BF16)
            sc[at] = scaled
            back = dot(scaled, w2[...], second) * (-scale)
            sig = jax.nn.sigmoid(f1)
            act = f1 * sig
            slope = sig * (1.0 + f1 * (1.0 - sig))
            hk[at] = (act * f3).astype(BF16)
            d1[at] = (back * f3 * slope).astype(BF16)
            d3[at] = (back * act).astype(BF16)
            return carry

        lax.fori_loop(0, tokens // step, forward, 0)
        for n, (lhs, rhs, by) in enumerate(((d1, k_ref, scale), (d3, k_ref, scale), (sc, hk, -scale))):
            grad[pl.ds(n * hidden, hidden)] = dot(lhs[...], rhs[...], TN) * by
        c = class_of(lax.axis_index("ctx"))
        send_ref[...] = grad[pl.ds(pl.multiple_of((1 - c) * half, 16), half)].astype(BF16)
        keep_ref[...] = grad[pl.ds(pl.multiple_of(c * half, 16), half)]

    def kernel(kv, rate_ref, *refs):
        w_in, refs = refs[:count], refs[count:]
        send_ref, keep_ref, *refs = refs
        hk, sc, d1, d3, grad, rate_col, sems, *refs = refs
        w_ref = w_in[0] if first_group else refs[0]
        rate_col[...] = jnp.broadcast_to(rate_ref[group], (8, tokens)).T
        if not first_group:
            wait(fetch(weight_pairs(w_in, w_ref, hidden, True), sems))
        body((send_ref, keep_ref, kv, w_ref, rate_ref, hk, sc, d1, d3, grad, rate_col))

    out_shape = [
        jax.ShapeDtypeStruct((half, width), BF16),
        jax.ShapeDtypeStruct((half, width), F32),
    ]
    scratch = [pltpu.VMEM((tokens, hidden), BF16) for _ in range(4)]
    scratch += [
        pltpu.VMEM((rows, width), F32),
        pltpu.VMEM((tokens, 8), F32),
        pltpu.SemaphoreType.DMA((2,)),
    ]
    operands = [kv, rates, *weights]
    in_specs = [VMEM] * len(operands)
    if not first_group:
        scratch.append(pltpu.VMEM((rows, width), BF16))
    return pl.pallas_call(
        kernel,
        in_specs=in_specs,
        out_specs=[VMEM] * len(out_shape),
        out_shape=out_shape,
        scratch_shapes=scratch,
        compiler_params=limit(12),
        name="key_side",
    )(*operands)


def side_by_side(keys, values, weights, group, singles):
    tokens, width = keys.shape[1:]
    count = len(weights)
    sources = [(0, group), (1, group), *singles]

    def kernel(*refs):
        kv_in, w_in, refs = refs[:2], refs[2 : 2 + count], refs[2 + count :]
        kv, targets, (*w_ref, sems, w_sems) = refs[0], refs[1 : 1 + len(singles)], refs[1 + len(singles) :]
        targets = (kv.at[0], kv.at[1], *targets)
        loads = fetch([(kv_in[n].at[g], to) for (n, g), to in zip(sources, targets)], sems)
        wait(loads + (fetch(weight_pairs(w_in, w_ref[0], width, False), w_sems) if count else []))

    out_shape = [jax.ShapeDtypeStruct((2, tokens, width), BF16)]
    out_shape += [jax.ShapeDtypeStruct((tokens, width), BF16)] * len(singles)
    if count:
        out_shape.append(jax.ShapeDtypeStruct((count * width, weights[0].shape[2]), BF16))
    return pl.pallas_call(
        kernel,
        in_specs=[HBM] * (2 + count),
        out_specs=[VMEM] * len(out_shape),
        out_shape=out_shape,
        scratch_shapes=[pltpu.SemaphoreType.DMA((len(sources),)), pltpu.SemaphoreType.DMA((3,))],
        compiler_params=limit(2),
        name="side_by_side",
    )(*in_hbm(keys, values, *weights))


def window_side(query, keys, values, chip, near, far, group):
    tokens, width = query.shape[1:]
    reach = WINDOW // 2
    total = tokens + WINDOW
    step = min(256, tokens)
    span = step + WINDOW
    scale = width ** (-0.5)

    def kernel(q_in, k_in, v_in, chip_ref, near_ref, *refs):
        far_refs, (out_ref, q_ref, k_all, v_all, sems, far_sems) = refs[:-6], refs[-6:]
        far_parts = far_refs if len(far_refs) == 2 else (far_refs[0].at[0], far_refs[0].at[1])
        index = lax.axis_index("ctx")
        core = index & 1
        other = class_of(index)
        chip_at = pl.ds(pl.multiple_of((1 - core) * (reach + tokens), 128), reach)
        far_at = pl.ds(pl.multiple_of(core * (reach + tokens), 128), reach)
        pairs = [(q_in.at[group], q_ref)]
        copies = []
        for n, (own_in, target) in enumerate(((k_in, k_all), (v_in, v_all))):
            pairs.append((own_in.at[group], target.at[pl.ds(reach, tokens)]))
            pairs.append((chip_ref.at[n], target.at[chip_at]))

            @pl.when(other == 1)
            def _():
                pltpu.make_async_copy(near_ref.at[n], target.at[far_at], far_sems.at[n]).start()

            @pl.when(other == 0)
            def _():
                pltpu.make_async_copy(far_parts[n], target.at[far_at], far_sems.at[n]).start()

            copies.append(pltpu.make_async_copy(near_ref.at[n], target.at[far_at], far_sems.at[n]))
        wait(fetch(pairs, sems) + copies)
        lowest = jnp.where(index == 0, reach, 0)
        highest = jnp.where(index == lax.axis_size("ctx") - 1, reach + tokens, total)

        def block(n, carry):
            start = n * step
            q = q_ref[pl.ds(start, step)]
            scores = dot(q, k_all[pl.ds(start, span)], NT) * scale
            row = lax.broadcasted_iota(jnp.int32, (step, span), 0)
            col = lax.broadcasted_iota(jnp.int32, (step, span), 1)
            valid = (
                (col >= row)
                & (col < row + WINDOW)
                & (col >= lowest - start)
                & (col < highest - start)
            )
            scores = jnp.where(valid, scores, -1e30)
            largest = jnp.max(scores, axis=1, keepdims=True)
            expo = jnp.exp(scores - largest)
            norm = jnp.sum(expo, axis=1, keepdims=True)
            mixed = dot(expo.astype(BF16), v_all[pl.ds(start, span)], NN)
            out_ref[pl.ds(start, step)] = mixed / norm
            return carry

        lax.fori_loop(0, tokens // step, block, 0)

    return pl.pallas_call(
        kernel,
        in_specs=[HBM] * (5 + len(far)),
        out_specs=VMEM,
        out_shape=jax.ShapeDtypeStruct((tokens, width), F32),
        scratch_shapes=[
            pltpu.VMEM((tokens, width), BF16),
            pltpu.VMEM((total, width), BF16),
            pltpu.VMEM((total, width), BF16),
            pltpu.SemaphoreType.DMA((5,)),
            pltpu.SemaphoreType.DMA((2,)),
        ],
        compiler_params=limit(12),
        name="window_side",
    )(*in_hbm(query, keys, values), chip, near, *far)


def query_side(query, gain, window, weights, group, gathered):
    tokens, width = query.shape[1:]
    hidden = width
    rows = 3 * hidden
    step = min(512, tokens)
    scale = width ** (-0.5)
    first = NT if gathered else NN
    count = len(weights)

    def kernel(q_in, gain_ref, window_ref, *refs):
        w_in, (out_ref, q_ref, w_ref, sems) = refs[:count], refs[count:]
        pairs = [(q_in.at[group], q_ref)]
        wait(fetch(pairs + weight_pairs(w_in, w_ref, hidden, gathered), sems))
        w1, w3, w2 = (w_ref.at[pl.ds(n * hidden, hidden)] for n in range(3))

        def block(n, carry):
            at = pl.ds(n * step, step)
            q = q_ref[at]
            g1 = dot(q, w1[...], first) * scale
            g3 = dot(q, w3[...], first) * scale
            hq = (g1 * jax.nn.sigmoid(g1) * g3).astype(BF16)
            ttt = dot(hq, w2[...], first) * scale
            mean = jnp.mean(ttt * ttt, axis=1, keepdims=True)
            normed = ttt * lax.rsqrt(mean + 1e-06) * gain_ref[...]
            out_ref[at] = (normed + window_ref[at]).astype(BF16)
            return carry

        lax.fori_loop(0, tokens // step, block, 0)

    return pl.pallas_call(
        kernel,
        in_specs=[HBM, VMEM, VMEM] + [VMEM if gathered else HBM] * count,
        out_specs=VMEM,
        out_shape=jax.ShapeDtypeStruct((tokens, width), BF16),
        scratch_shapes=[
            pltpu.VMEM((tokens, width), BF16),
            pltpu.VMEM((rows, width), BF16),
            pltpu.SemaphoreType.DMA((4,)),
        ],
        compiler_params=limit(10),
        name="query_side",
    )(*in_hbm(query), gain, window, *(weights if gathered else in_hbm(*weights)))


CALLS = 2


def tiles(features):
    tile = 512 if features % 512 == 0 else 128
    count = features // tile
    middle = (count + 1) // CALLS
    return tile, (range(middle), range(middle, count))


def project(heads, mine, near, far, group, call, mixed):
    tokens, width = heads[0].shape
    count = len(heads)
    part = width // 2
    features = mine.shape[1] // count
    tile, shares = tiles(features)
    share = shares[call]
    blocks = len(share)

    def kernel(*refs):
        head_refs, refs = refs[:count], refs[count:]
        mine_ref, refs = refs[0], refs[1:]
        near_refs, refs = refs[: count - 1], refs[count - 1 :]
        far_refs, refs = refs[: count - 1], refs[count - 1 :]
        out_ref, w_ref, done_ref, sems, out_sems = refs[-5:]
        c = lax.axis_index("ctx") & 1
        start = lax.axis_index("head") * features
        loads = fetch(
            [
                (mine_ref.at[:, pl.ds(pl.multiple_of(start + t * tile, 128), tile)], w_ref.at[n])
                for n, t in enumerate(share)
            ],
            sems,
        )
        stores = []
        for n, t in enumerate(share):
            at = pl.ds(t * tile, tile)
            total = None
            for head, one, two in zip(head_refs[1:], near_refs, far_refs):
                for source, half in ((one, c), (two, 1 - c)):
                    rows = head[:, pl.ds(pl.multiple_of(half * part, 128), part)]
                    term = dot(rows, source[:, at], NN)
                    total = term if total is None else total + term
            loads[n].wait()
            term = dot(head_refs[0][...], w_ref[n], NN)
            done_ref[n] = (term if total is None else total + term).astype(BF16)
            stores += fetch([(done_ref.at[n], out_ref.at[group, :, at])], out_sems.at[pl.ds(n, 1)])
        wait(stores)

    operands = [*heads, mine, *near, *far]
    in_specs = [VMEM] * count + [HBM] + [VMEM] * (2 * (count - 1))
    operands[count] = in_hbm(mine)[0]
    aliases = {}
    if mixed is not None:
        aliases = {len(operands): 0}
        operands.append(mixed)
        in_specs.append(HBM)
    return pl.pallas_call(
        kernel,
        in_specs=in_specs,
        out_specs=HBM,
        out_shape=jax.ShapeDtypeStruct((GROUPS, tokens, features), BF16),
        input_output_aliases=aliases,
        scratch_shapes=[
            pltpu.VMEM((blocks, width, tile), BF16),
            pltpu.VMEM((blocks, tokens, tile), BF16),
            pltpu.SemaphoreType.DMA((blocks,)),
            pltpu.SemaphoreType.DMA((blocks,)),
        ],
        compiler_params=limit(12),
        name="project",
    )(*operands)


def piece_for(weights, shift, heads):
    width, features = weights.shape
    part = width // 2
    features //= heads

    def kernel(in_ref, out_ref, sem):
        c = lax.axis_index("ctx") & 1
        target = (lax.axis_index("head") + shift) % heads
        rows = pl.ds(pl.multiple_of(c * part, 16), part)
        columns = pl.ds(pl.multiple_of(target * features, 128), features)
        wait(fetch([(in_ref.at[rows, columns], out_ref)], sem))

    return pl.pallas_call(
        kernel,
        in_specs=[HBM],
        out_specs=VMEM,
        out_shape=jax.ShapeDtypeStruct((part, features), weights.dtype),
        scratch_shapes=[pltpu.SemaphoreType.DMA((1,))],
        compiler_params=limit(2),
        name="piece_for",
    )(*in_hbm(weights))


def turned_half(rows_half, flip, outs):
    half, width = rows_half.shape
    part = half // 3
    hidden = 2 * part

    def kernel(*refs):
        in_ref, targets, (block_ref, sems) = refs[0], refs[-5:-2], refs[-2:]
        h = class_of(lax.axis_index("ctx"))
        if flip:
            h = 1 - h
        copies = []
        for j in range(3):
            block_ref[j] = in_ref[pl.ds(j * part, part)].T
            for value in range(2):
                matrix, side = divmod(3 * value + j, 2)
                place = targets[matrix].at[0, :, pl.ds(side * part, part)]
                copy = pltpu.make_async_copy(block_ref.at[j], place, sems.at[j])

                @pl.when(h == value)
                def _():
                    copy.start()

            copies.append(copy)
        wait(copies)

    return pl.pallas_call(
        kernel,
        in_specs=[VMEM] + [HBM] * len(outs),
        out_specs=[HBM] * 3,
        out_shape=[jax.ShapeDtypeStruct((1, width, hidden), BF16)] * 3,
        input_output_aliases={n + 1: n for n in range(len(outs))},
        scratch_shapes=[pltpu.VMEM((3, width, part), BF16), pltpu.SemaphoreType.DMA((3,))],
        compiler_params=limit(4),
        name="turned_half",
    )(rows_half, *outs)


def orders(count):
    rest = list(range(1, count.bit_length() - 1))
    return rest[1:] + rest[:1], rest


def class_of(index):
    return (index ^ (index >> 1)) & 1


def swap_pairs(count):
    return [(i, i ^ 1) for i in range(count)]


def mask(step_bit):
    return 3 if step_bit == 1 else 1 << step_bit


def exchange(value, count, step):
    ones, others = orders(count)
    pairs = [(i, i ^ mask((others if class_of(i) else ones)[step])) for i in range(count)]
    return lax.ppermute(value, "ctx", pairs)


def own_bit(index, count, step):
    ones, others = orders(count)
    return jnp.where(class_of(index) == 1, (index >> others[step]) & 1, (index >> ones[step]) & 1)


def piece_rows(refs, index, count, steps, flip):
    total = None
    for made, ref in enumerate(refs):
        start, rows = 0, ref.shape[0]
        for step in range(max(made - 1, 0), steps):
            rows //= 2
            bit = own_bit(index, count, step)
            start += (1 - bit if flip and step == steps - 1 else bit) * rows
        part = ref[...] if isinstance(start, int) else ref[pl.ds(pl.multiple_of(start, 16), rows)]
        total = part.astype(F32) if total is None else total + part.astype(F32)
    return total


def partial_sum(pieces, count, steps):
    rows, width = pieces[0].shape
    rows >>= steps

    def kernel(*refs):
        index = lax.axis_index("ctx")
        refs[-1][...] = piece_rows(refs[:-1], index, count, steps, True).astype(BF16)

    return pl.pallas_call(
        kernel,
        in_specs=[VMEM] * len(pieces),
        out_specs=VMEM,
        out_shape=jax.ShapeDtypeStruct((rows, width), BF16),
        compiler_params=limit(4),
        name="partial_sum",
    )(*pieces)


def renormed(before, pieces, count, steps):
    rows, width = before.shape

    def kernel(before_ref, *refs):
        index = lax.axis_index("ctx")
        old = before_ref[...]
        changed = old - piece_rows(refs[:-2], index, count, steps, False)
        kept = jnp.sqrt(jnp.sum(old * old, axis=1, keepdims=True))
        new = changed * (kept / jnp.sqrt(jnp.sum(changed * changed, axis=1, keepdims=True) + 1e-06))
        refs[-2][...] = new
        refs[-1][...] = new.astype(BF16)

    return pl.pallas_call(
        kernel,
        in_specs=[VMEM] * (1 + len(pieces)),
        out_specs=[VMEM] * 2,
        out_shape=[
            jax.ShapeDtypeStruct((rows, width), F32),
            jax.ShapeDtypeStruct((rows, width), BF16),
        ],
        compiler_params=limit(4),
        name="renormed",
    )(before, *pieces)


def next_state(before, send, keep, count):
    pieces = [keep, lax.ppermute(send, "ctx", swap_pairs(count))]
    steps = len(orders(count)[0])
    for step in range(steps):
        out = partial_sum(pieces, count, step + 1)
        pieces.append(exchange(out, count, step))
    return renormed(before, pieces, count, steps)


def joined(shard, got, count, step):
    rows, width = shard.shape

    def kernel(shard_ref, got_ref, out_ref):
        bit = own_bit(lax.axis_index("ctx"), count, step)
        out_ref[pl.ds(pl.multiple_of(bit * rows, 16), rows)] = shard_ref[...]
        out_ref[pl.ds(pl.multiple_of((1 - bit) * rows, 16), rows)] = got_ref[...]

    return pl.pallas_call(
        kernel,
        in_specs=[VMEM] * 2,
        out_specs=VMEM,
        out_shape=jax.ShapeDtypeStruct((2 * rows, width), shard.dtype),
        compiler_params=limit(4),
        name="joined",
    )(shard, got)


def gather_rows(shard, count):
    steps = len(orders(count)[0])
    for step in reversed(range(steps)):
        got = exchange(shard, count, step)
        shard = joined(shard, got, count, step)
    return shard, lax.ppermute(shard, "ctx", swap_pairs(count))


def row_start(index, count, rows):
    rows //= 2
    start = class_of(index) * rows
    for step in range(len(orders(count)[0])):
        rows //= 2
        start += own_bit(index, count, step) * rows
    return start


def own_rows(weights, count):
    width, hidden = weights[0].shape[1:]
    rows = 3 * hidden

    def kernel(*refs):
        w_in, (out_ref, w_ref, turned, sems) = refs[:3], refs[3:]
        wait(fetch(weight_pairs(w_in, w_ref, width, False), sems))
        for n in range(3):
            turned[pl.ds(n * hidden, hidden)] = w_ref[pl.ds(n * width, width)].T
        start = pl.multiple_of(row_start(lax.axis_index("ctx"), count, rows), 16)
        out_ref[...] = turned[pl.ds(start, rows // count)].astype(F32)

    return pl.pallas_call(
        kernel,
        in_specs=[HBM] * 3,
        out_specs=VMEM,
        out_shape=jax.ShapeDtypeStruct((rows // count, width), F32),
        scratch_shapes=[
            pltpu.VMEM((3 * width, hidden), BF16),
            pltpu.VMEM((rows, width), BF16),
            pltpu.SemaphoreType.DMA((3,)),
        ],
        compiler_params=limit(6),
        name="own_rows",
    )(*in_hbm(*weights))


def layer(query, key_in, value, rates, w_in, w_gate, w_out, norm_gain, proj_weight):
    count = lax.axis_size("ctx")
    heads = lax.axis_size("head")
    index = lax.axis_index("ctx").astype(jnp.int32)
    core = (index & 1).astype(jnp.int32)
    tokens, _ = query.shape[1:]
    reach = WINDOW // 2

    kv, keys_only, natural = side_by_side(key_in, value, (w_in, w_gate, w_out), 0, [(0, 0)])
    send, keep = key_side(kv, rates, [natural], 0)
    later, values_only = side_by_side(key_in, value, (), 1, [(1, 0)])

    across = [(i, i + 1 if i & 1 else i - 1) for i in range(1, count - 1)]
    near_pairs = [(i, j) for i, j in across if class_of(i)]
    far_pairs = [(i, j) for i, j in across if not class_of(i)]

    def edge(rows, at_end):
        axis = rows.ndim - 2
        if tokens == reach:
            return rows
        return lax.dynamic_slice_in_dim(rows, (tokens - reach) * at_end, reach, axis)

    halos = []
    for own, alone in ((kv, (keys_only, values_only)), (later, (later,))):
        chip = lax.ppermute(edge(own, 1 - core), "ctx", swap_pairs(count))
        near_halo = lax.ppermute(edge(own, core), "ctx", near_pairs)
        far_halo = []
        for rows in alone:
            far_halo.append(lax.ppermute(edge(rows, core), "ctx", far_pairs))
        halos.append((chip, near_halo, far_halo))

    near = []
    far = []
    for shift in range(1, heads):
        piece = piece_for(proj_weight, shift, heads)
        got = lax.ppermute(piece, "head", [(i, (i + shift) % heads) for i in range(heads)])
        near.append(got)
        far.append(lax.ppermute(got, "ctx", swap_pairs(count)))

    state = own_rows((w_in, w_gate, w_out), count)

    weights = (w_in, w_gate, w_out)
    mixed = None
    for group in range(GROUPS):
        gathered = group > 0
        if gathered:
            send, keep = key_side(later, rates, weights, group)
        window = window_side(query, key_in, value, *halos[group], group)
        head_out = query_side(query, norm_gain, window, weights, group, gathered)
        outs = [head_out]
        for shift in range(1, heads):
            outs.append(
                lax.ppermute(head_out, "head", [(i, (i + shift) % heads) for i in range(heads)])
            )
        for call in range(CALLS):
            mixed = project(outs, proj_weight, near, far, group, call, mixed)
        state, shard = next_state(state, send, keep, count)
        weights = gather_rows(shard, count)
    outs = ()
    for flip, rows_half in enumerate(weights):
        outs = turned_half(rows_half, flip, outs)
    return (mixed, *outs)


def solution(mesh):
    return jax.shard_map(
        layer,
        mesh=mesh,
        in_specs=(
            P(None, "ctx", "head"),
            P(None, "ctx", "head"),
            P(None, "ctx", "head"),
            P(None, "head", "ctx"),
            P("head", None, None),
            P("head", None, None),
            P("head", None, None),
            P("head", None),
            P("head", None),
        ),
        out_specs=(
            P(None, "ctx", "head"),
            P("head", None, None),
            P("head", None, None),
            P("head", None, None),
        ),
        check_vma=False,
    )
```
